32 devices in a mesh: grp: 2 (over y), slab: 4 (over z), head: 2 (over x), seq: 2 (over core).
Axes of the slice: x: 2, y: 2, z: 4, core: 2. Of those that a mesh axis runs over, the one named last changes fastest.
Arguments:
- queries: bfloat16 [1024, 5120], P(('grp', 'seq'), 'head'), parts along dimension 0, may hold values from -140 to 140
- query_gain: float32 [5120], P('head'), may hold values from 1.5 to 3
- cache_keys: bfloat16 [4096, 5120], P(('grp', 'slab'), 'head'), parts along dimension 0, may hold values from -120 to 120
- cache_values: bfloat16 [4096, 5120], P(('grp', 'slab'), 'head'), parts along dimension 0, may hold values from -6 to 6
- finished_keys: bfloat16 [1024, 5120], P(('grp', 'slab', 'seq'), 'head'), parts along dimension 0, may hold values from -6 to 6
- finished_values: bfloat16 [1024, 5120], P(('grp', 'slab', 'seq'), 'head'), parts along dimension 0, may hold values from -6 to 6
- new_keys: bfloat16 [1024, 5120], P(('grp', 'slab', 'seq'), 'head'), parts along dimension 0, may hold values from -6 to 6
- new_values: bfloat16 [1024, 5120], P(('grp', 'slab', 'seq'), 'head'), parts along dimension 0, may hold values from -6 to 6
- out_weight: bfloat16 [5120, 5120], P('head', 'slab'), may hold values from -0.25 to 0.25
- time_weight: float32 [256, 5120], P(None, ('slab', 'head')), may hold values from -0.375 to 0.375
- owner: int32 [2], P('grp'), parts along dimension 0, may hold values from 0 to 3
- step: int32 [2], P('grp'), parts along dimension 0, may hold values from 0 to 999
Outputs:
- branch: bfloat16 [1024, 5120], P(('grp', 'seq'), ('slab', 'head')), parts along dimension 0
The draws below stay inside these ranges and needn't reach their ends.
There are 2 independent parts, one for each index of `grp`. The reference program is written for one: setup_inputs(seed, part) draws one part's arguments, and reference() takes and returns one part's arrays. A program takes and returns all parts, laid end to end along the dimension named above; an argument that names none is the same for every part. Nothing has to cross between parts.
All inputs are finite; a program needn't handle non-finite values.
Results may differ from the reference program's by a relative error of at most 0.012.
Values may be sent and summed in bfloat16 or wider, within the bound.
No kernel may reach another device: no remote copies, remote signals or barrier semaphores. Data moves between devices by JAX's collectives and lax.ppermute only.
A program may use at most 64 MiB of HBM per device.

```python
import math
import jax
import jax.numpy as jnp
from jax import lax

D = 5120
HEADS = 40
HD = 128
FREQ = 256
SPAN = 512
CACHE = 2048
N_SLAB = 4


def draw_cache_keys(key, part):
    shape_pair = (SPAN * N_SLAB, HEADS * HD)
    entries = jnp.clip(jax.random.normal(jax.random.fold_in(key, 11), shape_pair, jnp.float32), -4.5, 4.5)
    return entries.astype(jnp.bfloat16)


def draw_queries(key, part):
    width_total = HEADS * HD
    shape_pair = (SPAN, width_total)
    row_scale = jnp.exp(jax.random.uniform(jax.random.fold_in(key, 21), (SPAN, 1), jnp.float32, jnp.log(0.5), jnp.log(5.0)))
    column_rise = 3.0 ** (jnp.arange(width_total, dtype=jnp.float32) / (width_total - 1))
    jitter = jnp.exp(jax.random.uniform(jax.random.fold_in(key, 22), (width_total,), jnp.float32, jnp.log(0.5), jnp.log(2.0)))
    entries = jnp.clip(jax.random.normal(jax.random.fold_in(key, 23), shape_pair, jnp.float32), -4.5, 4.5)
    entries = entries * row_scale * column_rise * jitter
    return entries.astype(jnp.bfloat16)


def shard_levels(key, shape, cuts, least, largest):
    gain, own = 1.0, jax.random.fold_in(key, 6)
    for axis_at, blocks in cuts:
        draws = jnp.exp(jax.random.uniform(jax.random.fold_in(own, axis_at), (blocks,), jnp.float32, least / len(cuts), largest / len(cuts)))
        gain = gain * jnp.repeat(draws, shape[axis_at] // blocks).reshape([-1 if axis == axis_at else 1 for axis in range(len(shape))])
    return gain


def bell_draw(rng, dims, width, bound, pieces=(), kind=jnp.bfloat16):
    values = width * jax.random.normal(rng, dims, jnp.float32)
    if pieces:
        values = values * shard_levels(rng, dims, pieces, -0.22, 0.18)
    return jnp.clip(values, -bound, bound).astype(kind)


def setup_inputs(seed: int = 0, part: int = 0) -> dict:
    arg_keys = jax.random.split(jax.random.key(seed), 13)
    own_keys = jax.random.split(jax.random.fold_in(arg_keys[12], part), 13)
    return {
        "queries": draw_queries(jax.random.fold_in(jax.random.fold_in(arg_keys[12], part), 71), part),
        "query_gain": jnp.clip(jnp.exp(math.log(3.0) - 0.6931472 * jax.random.uniform(arg_keys[1], (HEADS * HD,), jnp.float32) ** shard_levels(arg_keys[1], (HEADS * HD,), ((0, 2),), -0.2, 0.2)), 1.5, 3.0),
        "cache_keys": draw_cache_keys(jax.random.fold_in(jax.random.fold_in(arg_keys[12], part), 71), part),
        "cache_values": bell_draw(own_keys[3], (CACHE, HEADS * HD), 1.0, 6.0, ((0, 4), (1, 2))),
        "finished_keys": bell_draw(own_keys[4], (SPAN, HEADS * HD), 1.0, 6.0, ((0, 8), (1, 2))),
        "finished_values": bell_draw(own_keys[5], (SPAN, HEADS * HD), 1.0, 6.0, ((0, 8), (1, 2))),
        "new_keys": bell_draw(own_keys[6], (SPAN, HEADS * HD), 1.0, 6.0, ((0, 8), (1, 2))),
        "new_values": bell_draw(own_keys[7], (SPAN, HEADS * HD), 1.0, 6.0, ((0, 8), (1, 2))),
        "out_weight": bell_draw(arg_keys[8], (HEADS * HD, D), (HEADS * HD // 8) ** -0.5, 0.25, ((0, 2), (1, 4))),
        "time_weight": bell_draw(arg_keys[9], (FREQ, D), FREQ ** -0.5, 0.375, ((1, 8),), jnp.float32),
        "owner": jax.random.randint(own_keys[10], (1,), 0, N_SLAB).astype(jnp.int32),
        "step": jax.random.randint(own_keys[11], (1,), 0, 1000).astype(jnp.int32),
    }


EPSILON = 1e-06

def reference(queries, query_gain, cache_keys, cache_values, finished_keys, finished_values, new_keys, new_values, out_weight, time_weight, owner, step):
    query_float = queries.astype(jnp.float32)
    inverse = lax.rsqrt(lax.optimization_barrier(jnp.mean(query_float * query_float, axis=1)) + EPSILON)
    normed = (query_float * inverse[:, None] * query_gain).astype(jnp.bfloat16)
    start_row = (owner[0] * SPAN).astype(jnp.int32)
    swapped_keys = lax.dynamic_update_slice(cache_keys, finished_keys, (start_row, jnp.int32(0)))
    swapped_values = lax.dynamic_update_slice(cache_values, finished_values, (start_row, jnp.int32(0)))
    all_keys = jnp.concatenate([swapped_keys, new_keys], axis=0)
    all_values = jnp.concatenate([swapped_values, new_values], axis=0)
    total_rows = CACHE + SPAN
    query_heads = normed.reshape(SPAN, HEADS, HD).transpose(1, 0, 2)
    key_heads = all_keys.reshape(total_rows, HEADS, HD).transpose(1, 0, 2)
    value_heads = all_values.reshape(total_rows, HEADS, HD).transpose(1, 0, 2)
    score_scale = 1.0 / HD ** 0.5

    def one_head(head_items):
        query_head, key_head, value_head = head_items
        scores = jnp.dot(query_head, key_head.T, preferred_element_type=jnp.float32) * score_scale
        row_top = lax.optimization_barrier(jnp.max(scores, axis=1, keepdims=True))
        raw_weights = jnp.exp(scores - row_top)
        row_mass = lax.optimization_barrier(jnp.sum(raw_weights, axis=1, keepdims=True))
        weighted = jnp.dot(raw_weights.astype(jnp.bfloat16), value_head, preferred_element_type=jnp.float32)
        return (weighted / row_mass).astype(jnp.bfloat16)
    attended = lax.map(one_head, (query_heads, key_heads, value_heads))
    weight_heads = out_weight.reshape(HEADS, HD, D)
    projected = jnp.einsum('hrd,hdc->rc', attended.astype(jnp.float32), weight_heads.astype(jnp.float32))
    half = FREQ // 2
    frequency = jnp.exp(-jnp.log(10000.0) * jnp.arange(half, dtype=jnp.float32) / half)
    phases = step[0].astype(jnp.float32) * frequency
    embedding = jnp.concatenate([jnp.cos(phases), jnp.sin(phases)])
    time_gate = 1.0 + jnp.dot(embedding, time_weight, precision=lax.Precision.HIGHEST)
    return (time_gate * projected).astype(jnp.bfloat16)
```

```python
import functools

import jax
import jax.numpy as jnp
from jax import lax
from jax.experimental import pallas as pl
from jax.experimental.pallas import tpu as pltpu
from jax.sharding import PartitionSpec as P

HD = 128
EPSILON = 1e-06
LOG2E = 1.4426950408889634
OUT = -1e30
F32 = jnp.float32
BF16 = jnp.bfloat16
STATS = 16


def chunk_sizes(heads):
    if heads % 2 == 0 and heads >= 8:
        middle = heads - 4
        sizes = [2] + [4] * (middle // 4) + ([middle % 4] if middle % 4 else []) + [2]
        return sizes, 2
    return [1] * (heads % 2) + [2] * (heads // 2), 1


def square_kernel(q_ref, out_ref):
    heads = q_ref.shape[1] // HD
    total = None
    for h in range(heads):
        block = q_ref[:, h * HD : (h + 1) * HD].astype(F32)
        term = block * block
        total = term if total is None else total + term
    row = jnp.sum(total.T, axis=0, keepdims=True)
    out_ref[...] = jnp.broadcast_to(row, out_ref.shape)


def row_squares(queries):
    rows = queries.shape[0]
    return pl.pallas_call(
        square_kernel,
        out_shape=jax.ShapeDtypeStruct((8, rows), F32),
        cost_estimate=pl.CostEstimate(
            flops=2 * queries.size, bytes_accessed=2 * queries.size, transcendentals=0
        ),
        name="row_squares",
    )(queries)


def attend_kernel(
    unit, heads, width, owner_ref, q_ref, gain_ref, own_sq, far_sq, kc, vc, near, far,
    out_ref, inv_s, lse_s,
):
    step = pl.program_id(0)
    half = near.shape[0] // 2
    scale = LOG2E / HD**0.5

    @pl.when(step == 0)
    def _():
        total = own_sq[0:1, :] + far_sq[0:1, :]
        inverse = lax.rsqrt(total / width + EPSILON)
        inv_s[...] = jnp.broadcast_to(inverse, (HD, inverse.shape[1])).T
        lse_s[...] = jnp.zeros_like(lse_s)

    penalty = jnp.where(owner_ref[0] == 1, F32(OUT), F32(0.0))
    nt = (((1,), (1,)), ((), ()))
    tn = (((0,), (0,)), ((), ()))
    for j in range(unit):
        cols = slice(j * HD, (j + 1) * HD)
        normed = (q_ref[:, cols].astype(F32) * inv_s[...] * gain_ref[:, cols]).astype(BF16)
        parts = [
            (kc[:, cols], vc[:, cols], True),
            (near[:half, cols], near[half:, cols], False),
            (far[:half, cols], far[half:, cols], False),
        ]
        scores = [
            lax.dot_general(k, normed, nt, preferred_element_type=F32) for k, _, _ in parts
        ]
        top = None
        for s, (_, _, masked) in zip(scores, parts):
            t = jnp.max(s, axis=0, keepdims=True)
            if masked:
                t = t + penalty
            top = t if top is None else jnp.maximum(top, t)
        base = top * scale
        mass, value = None, None
        for s, (_, v, masked) in zip(scores, parts):
            shift = base - penalty if masked else base
            raw = jnp.exp2(s * scale - shift)
            part_mass = jnp.sum(raw, axis=0, keepdims=True)
            part = lax.dot_general(v, raw.astype(BF16), tn, preferred_element_type=F32)
            mass = part_mass if mass is None else mass + part_mass
            value = part if value is None else value + part
        at = step * unit + j
        out_ref[pl.ds(pl.multiple_of(at * HD, HD), HD), :] = (value * (1.0 / mass)).astype(BF16)
        lse_s[pl.ds(at, 1), :] = base + jnp.log2(mass)

    @pl.when(step == pl.num_programs(0) - 1)
    def _():
        lse = lse_s[0:heads, :]
        high = lse.astype(BF16).astype(F32)
        rest = lse - high
        mid = rest.astype(BF16).astype(F32)
        low = rest - mid
        pad = jnp.zeros((STATS - 3 * heads, lse.shape[1]), F32)
        out_ref[heads * HD :, :] = jnp.concatenate([high, mid, low, pad], axis=0).astype(BF16)


def attend(unit, start, heads, width, is_owner, queries, gain, own_sq, far_sq, kc, vc, near, far):
    rows = queries.shape[0]
    first = start // unit
    wide = unit * HD

    def col(array_rows):
        return pl.BlockSpec((array_rows, wide), lambda i, o: (0, first + i))

    def whole(shape):
        return pl.BlockSpec(shape, lambda i, o: (0, 0))

    keys = kc.shape[0] + near.shape[0]
    out_rows = heads * HD + STATS
    return pl.pallas_call(
        functools.partial(attend_kernel, unit, heads, width),
        out_shape=jax.ShapeDtypeStruct((out_rows, rows), BF16),
        grid_spec=pltpu.PrefetchScalarGridSpec(
            num_scalar_prefetch=1,
            grid=(heads // unit,),
            in_specs=[
                col(rows),
                col(1),
                whole(own_sq.shape),
                whole(far_sq.shape),
                col(kc.shape[0]),
                col(vc.shape[0]),
                col(near.shape[0]),
                col(far.shape[0]),
            ],
            out_specs=whole((out_rows, rows)),
            scratch_shapes=[pltpu.VMEM((rows, HD), F32), pltpu.VMEM((8, rows), F32)],
        ),
        cost_estimate=pl.CostEstimate(
            flops=16 * heads * rows * keys * HD,
            bytes_accessed=4 * heads * keys * HD,
            transcendentals=heads * rows * keys,
        ),
        name="attend",
    )(is_owner, queries, gain, own_sq, far_sq, kc, vc, near, far)


def decode(ref, heads):
    stats = ref[heads * HD :, :].astype(F32)
    return stats[:heads] + stats[heads : 2 * heads] + stats[2 * heads : 3 * heads]


def merge_kernel(heads, final, take_ref, own, got, out_ref):
    take = take_ref[0] == 1
    own_lse = decode(own, heads)
    got_lse = jnp.where(take, decode(got, heads), F32(OUT))
    top = jnp.maximum(own_lse, got_lse)
    own_w = jnp.exp2(own_lse - top)
    got_w = jnp.exp2(got_lse - top)
    mass = own_w + got_w
    share = 1.0 / mass
    own_w, got_w = own_w * share, got_w * share
    for h in range(heads):
        at = slice(h * HD, (h + 1) * HD)
        mixed = own[at, :].astype(F32) * own_w[h : h + 1] + got[at, :].astype(F32) * got_w[h : h + 1]
        out_ref[at, :] = mixed.astype(BF16)
    if not final:
        lse = top + jnp.log2(mass)
        high = lse.astype(BF16).astype(F32)
        rest = lse - high
        mid = rest.astype(BF16).astype(F32)
        low = rest - mid
        pad = jnp.zeros((STATS - 3 * heads, lse.shape[1]), F32)
        out_ref[heads * HD :, :] = jnp.concatenate([high, mid, low, pad], axis=0).astype(BF16)


def merge(heads, final, take, own, got):
    rows = own.shape[1]
    out_rows = heads * HD if final else heads * HD + STATS
    spec = pl.BlockSpec(memory_space=pltpu.VMEM)
    return pl.pallas_call(
        functools.partial(merge_kernel, heads, final),
        out_shape=jax.ShapeDtypeStruct((out_rows, rows), BF16),
        in_specs=[pl.BlockSpec(memory_space=pltpu.SMEM), spec, spec],
        out_specs=spec,
        cost_estimate=pl.CostEstimate(
            flops=4 * own.size, bytes_accessed=6 * own.size, transcendentals=0
        ),
        name="merge",
    )(take, own, got)


def local(
    n_slab, n_head, n_seq,
    queries, query_gain, cache_keys, cache_values, finished_keys, finished_values,
    new_keys, new_values, out_weight, time_weight, owner, step,
):
    heads = queries.shape[1] // HD
    width = queries.shape[1] * n_head
    slab = lax.axis_index("slab")

    near = jnp.concatenate([finished_keys, new_keys, finished_values, new_values], axis=0)
    if n_seq == 2:
        far = lax.ppermute(near, "seq", [(0, 1), (1, 0)])
    own_sq = row_squares(queries)
    if n_head == 2:
        far_sq = lax.ppermute(own_sq, "head", [(0, 1), (1, 0)])
    else:
        far_sq = lax.psum(own_sq, "head")
        own_sq = jnp.zeros_like(own_sq)
    is_owner = (slab == owner).astype(jnp.int32)
    gain = query_gain[None, :]

    sizes, unit = chunk_sizes(heads)
    starts = [sum(sizes[:c]) for c in range(len(sizes))]
    side = n_slab // 2
    projected = jnp.zeros((queries.shape[0], out_weight.shape[1]), F32)
    for start, size in zip(starts, sizes):
        own = attend(
            unit, start, size, width, is_owner, queries, gain, own_sq, far_sq,
            cache_keys, cache_values, near, far,
        )
        for j in range(side - 1):
            got = lax.ppermute(own, "slab", [(j, j + 1), (n_slab - 1 - j, n_slab - 2 - j)])
            take = ((slab == j + 1) | (slab == n_slab - 2 - j)).astype(jnp.int32)[None]
            own = merge(size, False, take, own, got)
        got = lax.ppermute(own, "slab", [(side - 1, side), (side, side - 1)])
        take = jnp.ones((1,), jnp.int32)
        attended = merge(size, True, take, own, got)
        for j in range(side - 2, -1, -1):
            got = lax.ppermute(attended, "slab", [(j + 1, j), (n_slab - 2 - j, n_slab - 1 - j)])
            attended = jnp.where((slab == j) | (slab == n_slab - 1 - j), got, attended)
        block = out_weight[start * HD : (start + size) * HD]
        projected = projected + lax.dot_general(
            attended, block, (((0,), (0,)), ((), ())), preferred_element_type=F32
        )

    half = time_weight.shape[0] // 2
    frequency = jnp.exp(-jnp.log(10000.0) * jnp.arange(half, dtype=F32) / half)
    phases = step[0].astype(F32) * frequency
    embedding = jnp.concatenate([jnp.cos(phases), jnp.sin(phases)])
    time_gate = 1.0 + jnp.dot(embedding, time_weight, precision=lax.Precision.HIGHEST)

    cols = time_weight.shape[1]
    if n_head == 2:
        me = lax.axis_index("head")
        left, right = projected[:, :cols], projected[:, cols:]
        kept = jnp.where(me == 0, left, right)
        sent = jnp.where(me == 0, right, left).astype(BF16)
        summed = kept + lax.ppermute(sent, "head", [(0, 1), (1, 0)]).astype(F32)
    else:
        summed = lax.psum_scatter(projected, "head", scatter_dimension=1, tiled=True)
    return (time_gate * summed).astype(BF16)


def solution(mesh):
    in_specs = (
        P(("grp", "seq"), "head"),
        P("head"),
        P(("grp", "slab"), "head"),
        P(("grp", "slab"), "head"),
        P(("grp", "slab", "seq"), "head"),
        P(("grp", "slab", "seq"), "head"),
        P(("grp", "slab", "seq"), "head"),
        P(("grp", "slab", "seq"), "head"),
        P("head", "slab"),
        P(None, ("slab", "head")),
        P("grp"),
        P("grp"),
    )
    out_specs = P(("grp", "seq"), ("slab", "head"))
    body = functools.partial(local, mesh.shape["slab"], mesh.shape["head"], mesh.shape["seq"])
    return jax.shard_map(body, mesh=mesh, in_specs=in_specs, out_specs=out_specs, check_vma=False)
```

```python
import functools

import jax
import jax.numpy as jnp
from jax import lax
from jax.experimental import pallas as pl
from jax.experimental.pallas import tpu as pltpu
from jax.sharding import PartitionSpec as P

HD = 128
EPSILON = 1e-06
LOG2E = 1.4426950408889634
OUT = -1e30
F32 = jnp.float32
BF16 = jnp.bfloat16
STATS = 16


def chunk_sizes(heads):
    count = -(-heads // 4)
    return [heads // count + (c < heads % count) for c in range(count)]


def in_order(value, *earlier):
    return lax.optimization_barrier((value, *earlier))[0]


def vmem():
    return pl.BlockSpec(memory_space=pltpu.VMEM)


def hbm():
    return pl.BlockSpec(memory_space=pltpu.HBM)


def in_hbm(*arrays):
    return [pltpu.with_memory_space_constraint(array, pltpu.HBM) for array in arrays]


def prepare_kernel(q_hbm, fk, nk, fv, nv, squares_ref, near_ref, q_ref, sems):
    rows = fk.shape[0]
    copies = [pltpu.make_async_copy(q_hbm, q_ref, sems.at[0])] + [
        pltpu.make_async_copy(src, near_ref.at[pl.ds(n * rows, rows), :], sems.at[n + 1])
        for n, src in enumerate((fk, nk, fv, nv))
    ]
    for copy in copies:
        copy.start()
    copies[0].wait()
    total = None
    for h in range(q_ref.shape[1] // HD):
        block = q_ref[:, h * HD : (h + 1) * HD].astype(F32)
        term = block * block
        total = term if total is None else total + term
    row = jnp.sum(total.T, axis=0, keepdims=True)
    squares_ref[...] = jnp.broadcast_to(row, squares_ref.shape)
    for copy in copies[1:]:
        copy.wait()


def prepare(queries, fk, nk, fv, nv):
    rows = queries.shape[0]
    return pl.pallas_call(
        prepare_kernel,
        out_shape=(
            jax.ShapeDtypeStruct((8, rows), F32),
            jax.ShapeDtypeStruct((4 * fk.shape[0], fk.shape[1]), BF16),
        ),
        in_specs=[hbm()] * 5,
        out_specs=(vmem(), vmem()),
        scratch_shapes=[pltpu.VMEM(queries.shape, BF16), pltpu.SemaphoreType.DMA((5,))],
        cost_estimate=pl.CostEstimate(
            flops=2 * queries.size, bytes_accessed=8 * queries.size, transcendentals=0
        ),
        compiler_params=pltpu.CompilerParams(vmem_limit_bytes=8 << 20),
        name="prepare",
    )(queries, fk, nk, fv, nv)


NT = (((1,), (1,)), ((), ()))
TN = (((0,), (0,)), ((), ()))


def attend_kernel(
    start, heads, width, owner_ref, gain_hbm, own_hbm, far_sq_hbm, q_hbm, kc_hbm, vc_hbm, near_hbm,
    far_hbm, out_ref, lse_s, s_a, s_b, p_a, p_b, gain_ref, own_sq, far_sq, q_ref, kc, vc, near,
    far, small_sems, sems,
):
    half = near.shape[0] // 2
    cached = kc.shape[0]
    scale = LOG2E / HD**0.5
    sources = (q_hbm, kc_hbm, near_hbm, far_hbm, vc_hbm)
    mine = slice(start * HD, (start + heads) * HD)
    small = [
        pltpu.make_async_copy(own_hbm, own_sq, small_sems.at[0]),
        pltpu.make_async_copy(far_sq_hbm, far_sq, small_sems.at[1]),
        pltpu.make_async_copy(gain_hbm.at[:, mine], gain_ref, small_sems.at[2]),
    ]
    for copy in small:
        copy.start()
    copies = []
    for h in range(heads):
        here, there = slice(h * HD, (h + 1) * HD), slice((start + h) * HD, (start + h + 1) * HD)
        copies.append(
            [
                pltpu.make_async_copy(src.at[:, there], dst.at[:, here], sems.at[h, n])
                for n, (src, dst) in enumerate(zip(sources, (q_ref, kc, near, far, vc)))
            ]
        )
        for copy in copies[h]:
            copy.start()
    for copy in small:
        copy.wait()
    total = own_sq[0:1, :] + far_sq[0:1, :]
    inverse = lax.rsqrt(total / width + EPSILON)
    inverse = jnp.broadcast_to(inverse, (HD, inverse.shape[1])).T
    penalty = jnp.where(owner_ref[0] == 1, F32(OUT), F32(0.0))
    s_refs, p_refs = (s_a, s_b), (p_a, p_b)
    spans = [(0, cached), (cached, half), (cached + half, half)]
    masses = {}

    def score(h):
        for copy in copies[h]:
            copy.wait()
        cols = slice(h * HD, (h + 1) * HD)
        normed = (q_ref[:, cols].astype(F32) * inverse * gain_ref[:, cols]).astype(BF16)
        for (at, size), k in zip(spans, (kc[:, cols], near[:half, cols], far[:half, cols])):
            s_refs[h % 2][at : at + size, :] = lax.dot_general(
                k, normed, NT, preferred_element_type=F32
            )

    def soften(h):
        s_ref, p_ref = s_refs[h % 2], p_refs[h % 2]
        top = jnp.max(s_ref[:cached, :], axis=0, keepdims=True) + penalty
        top = jnp.maximum(top, jnp.max(s_ref[cached:, :], axis=0, keepdims=True))
        base = top * scale
        old = jnp.exp2(s_ref[:cached, :] * scale - (base - penalty))
        p_ref[:cached, :] = old.astype(BF16)
        new = jnp.exp2(s_ref[cached:, :] * scale - base)
        p_ref[cached:, :] = new.astype(BF16)
        mass = jnp.sum(old, axis=0, keepdims=True) + jnp.sum(new, axis=0, keepdims=True)
        masses[h] = mass
        lse_s[h : h + 1, :] = base + jnp.log2(mass)

    def gather(h):
        cols = slice(h * HD, (h + 1) * HD)
        value = None
        for (at, size), v in zip(spans, (vc[:, cols], near[half:, cols], far[half:, cols])):
            part = lax.dot_general(
                v, p_refs[h % 2][at : at + size, :], TN, preferred_element_type=F32
            )
            value = part if value is None else value + part
        out_ref[h * HD : (h + 1) * HD, :] = (value * (1.0 / masses[h])).astype(BF16)

    for t in range(heads + 2):
        if 0 <= t - 2:
            gather(t - 2)
        if 0 <= t - 1 < heads:
            soften(t - 1)
        if t < heads:
            score(t)
    out_ref[heads * HD :, :] = split(lse_s[0:heads, :])


def split(lse):
    high = lse.astype(BF16).astype(F32)
    rest = lse - high
    mid = rest.astype(BF16).astype(F32)
    low = rest - mid
    pad = jnp.zeros((STATS - 3 * lse.shape[0], lse.shape[1]), F32)
    return jnp.concatenate([high, mid, low, pad], axis=0).astype(BF16)


def attend(start, heads, width, is_owner, queries, gain, own_sq, far_sq, kc, vc, near, far):
    rows = queries.shape[0]
    keys = kc.shape[0] + near.shape[0]
    wide = heads * HD
    return pl.pallas_call(
        functools.partial(attend_kernel, start, heads, width),
        out_shape=jax.ShapeDtypeStruct((wide + STATS, rows), BF16),
        in_specs=[pl.BlockSpec(memory_space=pltpu.SMEM)] + [hbm()] * 8,
        out_specs=vmem(),
        scratch_shapes=[pltpu.VMEM((8, rows), F32)]
        + [pltpu.VMEM((keys, rows), F32)] * 2
        + [pltpu.VMEM((keys, rows), BF16)] * 2
        + [pltpu.VMEM((1, wide), F32), pltpu.VMEM((8, rows), F32), pltpu.VMEM((8, rows), F32)]
        + [pltpu.VMEM((array.shape[0], wide), BF16) for array in (queries, kc, vc, near, far)]
        + [pltpu.SemaphoreType.DMA((3,))]
        + [pltpu.SemaphoreType.DMA((heads, 5))],
        cost_estimate=pl.CostEstimate(
            flops=16 * heads * rows * keys * HD,
            bytes_accessed=4 * heads * keys * HD,
            transcendentals=heads * rows * keys,
        ),
        compiler_params=pltpu.CompilerParams(vmem_limit_bytes=12 << 20),
        name="attend",
    )(is_owner, gain, own_sq, far_sq, queries, kc, vc, near, far)


def stats_of(ref, heads):
    stats = ref[heads * HD :, :].astype(F32)
    return stats[:heads] + stats[heads : 2 * heads] + stats[2 * heads : 3 * heads]


def merge_kernel(heads, guarded, *refs):
    own, got, out_ref = refs[-3:]
    own_lse, got_lse = stats_of(own, heads), stats_of(got, heads)
    if guarded:
        got_lse = jnp.where(refs[0][0] == 1, got_lse, F32(OUT))
    top = jnp.maximum(own_lse, got_lse)
    own_w, got_w = jnp.exp2(own_lse - top), jnp.exp2(got_lse - top)
    mass = own_w + got_w
    share = 1.0 / mass
    own_w, got_w = own_w * share, got_w * share
    for h in range(heads):
        at = slice(h * HD, (h + 1) * HD)
        mixed = own[at, :].astype(F32) * own_w[h : h + 1] + got[at, :].astype(F32) * got_w[h : h + 1]
        out_ref[at, :] = mixed.astype(BF16)
    out_ref[heads * HD :, :] = split(top + jnp.log2(mass))


def merge(heads, take, own, got):
    guard = [] if take is None else [take.astype(jnp.int32)[None]]
    return pl.pallas_call(
        functools.partial(merge_kernel, heads, bool(guard)),
        out_shape=jax.ShapeDtypeStruct(own.shape, BF16),
        in_specs=[pl.BlockSpec(memory_space=pltpu.SMEM)] * len(guard) + [vmem()] * 2,
        out_specs=vmem(),
        cost_estimate=pl.CostEstimate(
            flops=4 * own.size, bytes_accessed=6 * own.size, transcendentals=0
        ),
        compiler_params=pltpu.CompilerParams(vmem_limit_bytes=4 << 20),
        name="merge",
    )(*guard, own, got)


def local(
    n_slab, n_head, n_seq,
    queries, query_gain, cache_keys, cache_values, finished_keys, finished_values,
    new_keys, new_values, out_weight, time_weight, owner, step,
):
    queries, cache_keys, cache_values, finished_keys, finished_values, new_keys, new_values = in_hbm(
        queries, cache_keys, cache_values, finished_keys, finished_values, new_keys, new_values
    )
    heads = queries.shape[1] // HD
    width = queries.shape[1] * n_head
    slab = lax.axis_index("slab")

    own_sq, near = prepare(queries, finished_keys, new_keys, finished_values, new_values)
    if n_head == 2:
        far_sq = lax.ppermute(own_sq, "head", [(0, 1), (1, 0)])
    else:
        far_sq = lax.psum(own_sq, "head")
        own_sq = jnp.zeros_like(own_sq)
    far = lax.ppermute(near, "seq", [(0, 1), (1, 0)])
    is_owner = (slab == owner).astype(jnp.int32)
    gain = query_gain[None, :]
    gain, own_sq, far_sq, near, far = in_hbm(gain, own_sq, far_sq, near, far)

    sizes = chunk_sizes(heads)
    starts = [sum(sizes[:c]) for c in range(len(sizes))]
    count = len(sizes)
    side = n_slab // 2
    lag = 3
    outer = functools.reduce(jnp.logical_or, [(slab < side - 1), (slab > side)])
    inward = [
        [(j, j + 1), (n_slab - 1 - j, n_slab - 2 - j)] for j in range(side - 1)
    ]
    outward = [[(b, a) for a, b in pairs] for pairs in inward]
    own, got_in, folded, crossed, total, final = {}, {}, {}, {}, {}, {}
    last = []

    def run(value):
        last[:] = [value]
        return value

    def attention(c):
        own[c] = run(
            attend(
                starts[c], sizes[c], width, in_order(is_owner, *last), queries, gain, own_sq,
                far_sq, cache_keys, cache_values, near, far,
            )
        )

    def send_in(c):
        sent = own[c]
        for j in range(side - 2):
            got = lax.ppermute(sent, "slab", inward[j])
            take = (slab == j + 1) | (slab == n_slab - 2 - j)
            sent = merge(sizes[c], take, sent, got)
        own[c] = sent
        got_in[c] = lax.ppermute(sent, "slab", inward[side - 2]) if side > 1 else sent

    def fold(c):
        take = ((slab == side - 1) | (slab == side)) if side != 2 else None
        folded[c] = run(merge(sizes[c], take, own[c], in_order(got_in[c], *last)))
        crossed[c] = lax.ppermute(folded[c], "slab", [(side - 1, side), (side, side - 1)])

    def cross(c):
        total[c] = run(merge(sizes[c], None, folded[c], in_order(crossed[c], *last)))

    def send_out(c):
        attended = total[c][: sizes[c] * HD]
        for j in range(side - 2, -1, -1):
            got = lax.ppermute(attended, "slab", outward[j])
            attended = jnp.where((slab == j) | (slab == n_slab - 1 - j), got, attended)
        final[c] = attended

    for t in range(count):
        attention(t)
        back = t - lag
        if back >= 0:
            cross(back)
        if side == 2 and back >= 0 and sizes[t] == sizes[back]:
            sent = jnp.where(outer, own[t], total[back])
            got = lax.ppermute(sent, "slab", inward[0] + outward[0])
            got_in[t] = got
            final[back] = jnp.where(outer, got, sent)[: sizes[back] * HD]
        else:
            send_in(t)
            if back >= 0:
                send_out(back)
        if t >= 1:
            fold(t - 1)
    fold(count - 1)
    for c in range(max(0, count - lag), count):
        cross(c)
        send_out(c)
    attended = jnp.concatenate([final[c] for c in range(count)], axis=0)
    projected = lax.dot_general(attended, out_weight, TN, preferred_element_type=F32)

    half = time_weight.shape[0] // 2
    frequency = jnp.exp(-jnp.log(10000.0) * jnp.arange(half, dtype=F32) / half)
    phases = step[0].astype(F32) * frequency
    embedding = jnp.concatenate([jnp.cos(phases), jnp.sin(phases)])
    time_gate = 1.0 + jnp.dot(embedding, time_weight, precision=lax.Precision.HIGHEST)

    cols = time_weight.shape[1]
    if n_head == 2:
        me = lax.axis_index("head")
        left, right = projected[:, :cols], projected[:, cols:]
        kept = jnp.where(me == 0, left, right)
        sent = jnp.where(me == 0, right, left).astype(BF16)
        summed = kept + lax.ppermute(sent, "head", [(0, 1), (1, 0)]).astype(F32)
    else:
        summed = lax.psum_scatter(projected, "head", scatter_dimension=1, tiled=True)
    return (time_gate * summed).astype(BF16)


def solution(mesh):
    in_specs = (
        P(("grp", "seq"), "head"),
        P("head"),
        P(("grp", "slab"), "head"),
        P(("grp", "slab"), "head"),
        P(("grp", "slab", "seq"), "head"),
        P(("grp", "slab", "seq"), "head"),
        P(("grp", "slab", "seq"), "head"),
        P(("grp", "slab", "seq"), "head"),
        P("head", "slab"),
        P(None, ("slab", "head")),
        P("grp"),
        P("grp"),
    )
    out_specs = P(("grp", "seq"), ("slab", "head"))
    body = functools.partial(local, mesh.shape["slab"], mesh.shape["head"], mesh.shape["seq"])
    return jax.shard_map(body, mesh=mesh, in_specs=in_specs, out_specs=out_specs, check_vma=False)
```

```python
import functools

import jax
import jax.numpy as jnp
from jax import lax
from jax.experimental import pallas as pl
from jax.experimental.pallas import tpu as pltpu
from jax.sharding import PartitionSpec as P


HD = 128
EPSILON = 1e-06
LOG2E = 1.4426950408889634
OUT = -1e30
F32 = jnp.float32
BF16 = jnp.bfloat16
STATS = 16


def chunk_sizes(heads):
    count = -(-heads // 5) if heads > 5 else 2
    return [heads // count + (c < heads % count) for c in range(count)]


def order_of(count):
    if count < 3:
        steps = [(kind, c) for c in range(count) for kind in "AI"]
        steps += [("F", c) for c in range(count)]
        return steps + [(kind, c) for c in range(count) for kind in "CO"]
    steps = [(kind, c) for c in range(count - 1) for kind in "AI"]
    steps += [("F", 0), ("A", count - 1), ("F", 1), ("C", 0), ("X", 0)]
    for c in range(2, count):
        steps += [("F", c), ("C", c - 1), ("O", c - 1)]
    return steps + [("C", count - 1), ("O", count - 1)]


def in_order(value, *earlier):
    return lax.optimization_barrier((value, *earlier))[0]


def vmem():
    return pl.BlockSpec(memory_space=pltpu.VMEM)


def hbm():
    return pl.BlockSpec(memory_space=pltpu.HBM)


def in_hbm(*arrays):
    return [pltpu.with_memory_space_constraint(array, pltpu.HBM) for array in arrays]


def prepare_kernel(q_hbm, fk, nk, fv, nv, squares_ref, near_ref, q_ref, sems):
    rows = fk.shape[0]
    copies = [pltpu.make_async_copy(q_hbm, q_ref, sems.at[0])] + [
        pltpu.make_async_copy(src, near_ref.at[pl.ds(n * rows, rows), :], sems.at[n + 1])
        for n, src in enumerate((fk, nk, fv, nv))
    ]
    for copy in copies:
        copy.start()
    copies[0].wait()
    total = None
    for h in range(q_ref.shape[1] // HD):
        block = q_ref[:, h * HD : (h + 1) * HD].astype(F32)
        term = block * block
        total = term if total is None else total + term
    row = jnp.sum(total.T, axis=0, keepdims=True)
    squares_ref[...] = jnp.broadcast_to(row, squares_ref.shape)
    for copy in copies[1:]:
        copy.wait()


def prepare(queries, fk, nk, fv, nv):
    rows = queries.shape[0]
    return pl.pallas_call(
        prepare_kernel,
        out_shape=(
            jax.ShapeDtypeStruct((8, rows), F32),
            jax.ShapeDtypeStruct((4 * fk.shape[0], fk.shape[1]), BF16),
        ),
        in_specs=[hbm()] * 5,
        out_specs=(vmem(), vmem()),
        scratch_shapes=[pltpu.VMEM(queries.shape, BF16), pltpu.SemaphoreType.DMA((5,))],
        cost_estimate=pl.CostEstimate(
            flops=2 * queries.size, bytes_accessed=8 * queries.size, transcendentals=0
        ),
        compiler_params=pltpu.CompilerParams(vmem_limit_bytes=8 << 20),
        name="prepare",
    )(queries, fk, nk, fv, nv)


NT = (((1,), (1,)), ((), ()))
TN = (((0,), (0,)), ((), ()))


def tiles_of(keys, cached, size=256):
    tiles, at = [], 0
    for end in (cached, keys):
        while at < end:
            step = min(size, end - at)
            tiles.append((at, step, end == cached))
            at += step
    return tiles


def by_eight(op, array):
    return op(array.reshape(array.shape[0] // 8, 8, array.shape[1]), axis=0)


def attend_kernel(
    start, heads, width, owner_ref, own_sq, far_sq, gain_hbm, q_hbm, kc_hbm, vc_hbm, near_hbm,
    far_hbm, out_ref, lse_s, s_a, s_b, p_a, p_b, gain_ref, q_ref, k_ref, v_ref, sems,
):
    half = near_hbm.shape[0] // 2
    cached, keys = kc_hbm.shape[0], k_ref.shape[0]
    scale = LOG2E / HD**0.5
    moves = [
        (gain_hbm, 0, gain_hbm.shape[0], gain_ref, 0),
        (q_hbm, 0, q_hbm.shape[0], q_ref, 0),
        (kc_hbm, 0, cached, k_ref, 0),
        (near_hbm, 0, half, k_ref, cached),
        (far_hbm, 0, half, k_ref, cached + half),
        (vc_hbm, 0, cached, v_ref, 0),
        (near_hbm, half, half, v_ref, cached),
        (far_hbm, half, half, v_ref, cached + half),
    ]
    groups = [(0, 1), (1, heads)] if heads > 1 else [(0, 1)]
    copies = []
    for g, (low, high) in enumerate(groups):
        here = slice(low * HD, high * HD)
        there = slice((start + low) * HD, (start + high) * HD)
        copies.append(
            [
                pltpu.make_async_copy(
                    src.at[at : at + size, there], dst.at[to : to + size, here], sems.at[g, n]
                )
                for n, (src, at, size, dst, to) in enumerate(moves)
            ]
        )
        for copy in copies[g]:
            copy.start()
    total = own_sq[0:1, :] + far_sq[0:1, :]
    inverse = lax.rsqrt(total / width + EPSILON)
    inverse = jnp.broadcast_to(inverse, (HD, inverse.shape[1])).T
    penalty = jnp.where(owner_ref[0] == 1, F32(OUT), F32(0.0))
    s_refs, p_refs = (s_a, s_b), (p_a, p_b)
    tiles = tiles_of(keys, cached)
    bases, masses = {}, {}
    for t in range(heads + 2):
        to_score, to_soften, to_gather = t, t - 1, t - 2
        scoring, softening, gathering = t < heads, 0 <= t - 1 < heads, t - 2 >= 0
        if t < len(groups):
            for copy in copies[t]:
                copy.wait()
        if scoring:
            cols = slice(to_score * HD, (to_score + 1) * HD)
            normed = (q_ref[:, cols].astype(F32) * inverse * gain_ref[:, cols]).astype(BF16)
            top = None
        value, mass = None, None
        for at, size, masked in tiles:
            span = slice(at, at + size)
            if gathering:
                part = lax.dot_general(
                    v_ref[span, to_gather * HD : (to_gather + 1) * HD],
                    p_refs[to_gather % 2][span, :],
                    TN,
                    preferred_element_type=F32,
                )
                value = part if value is None else value + part
            if scoring:
                scores = lax.dot_general(k_ref[span, cols], normed, NT, preferred_element_type=F32)
                s_refs[to_score % 2][span, :] = scores
                most = by_eight(jnp.max, scores)
                if masked:
                    most = most + penalty
                top = most if top is None else jnp.maximum(top, most)
            if softening:
                base = bases[to_soften]
                shift = base - penalty if masked else base
                raw = jnp.exp2(s_refs[to_soften % 2][span, :] * scale - shift)
                p_refs[to_soften % 2][span, :] = raw.astype(BF16)
                sums = by_eight(jnp.sum, raw)
                mass = sums if mass is None else mass + sums
        if gathering:
            at = slice(to_gather * HD, (to_gather + 1) * HD)
            out_ref[at, :] = (value * (1.0 / masses[to_gather])).astype(BF16)
        if softening:
            mass = jnp.sum(mass, axis=0, keepdims=True)
            masses[to_soften] = mass
            lse_s[to_soften : to_soften + 1, :] = bases[to_soften] + jnp.log2(mass)
        if scoring:
            bases[to_score] = jnp.max(top, axis=0, keepdims=True) * scale
    out_ref[heads * HD :, :] = split(lse_s[0:heads, :])


def split(lse):
    high = lse.astype(BF16).astype(F32)
    rest = lse - high
    mid = rest.astype(BF16).astype(F32)
    low = rest - mid
    pad = jnp.zeros((STATS - 3 * lse.shape[0], lse.shape[1]), F32)
    return jnp.concatenate([high, mid, low, pad], axis=0).astype(BF16)


def attend(start, heads, width, is_owner, queries, gain, own_sq, far_sq, kc, vc, near, far):
    rows = queries.shape[0]
    keys = kc.shape[0] + near.shape[0]
    wide = heads * HD
    return pl.pallas_call(
        functools.partial(attend_kernel, start, heads, width),
        out_shape=jax.ShapeDtypeStruct((wide + STATS, rows), BF16),
        in_specs=[pl.BlockSpec(memory_space=pltpu.SMEM)] + [vmem()] * 2 + [hbm()] * 6,
        out_specs=vmem(),
        scratch_shapes=[pltpu.VMEM((8, rows), F32)]
        + [pltpu.VMEM((keys, rows), F32)] * 2
        + [pltpu.VMEM((keys, rows), BF16)] * 2
        + [pltpu.VMEM((1, wide), F32), pltpu.VMEM((rows, wide), BF16)]
        + [pltpu.VMEM((keys, wide), BF16)] * 2
        + [pltpu.SemaphoreType.DMA((2, 8))],
        cost_estimate=pl.CostEstimate(
            flops=16 * heads * rows * keys * HD,
            bytes_accessed=4 * heads * keys * HD,
            transcendentals=heads * rows * keys,
        ),
        compiler_params=pltpu.CompilerParams(vmem_limit_bytes=12 << 20),
        name="attend",
    )(is_owner, own_sq, far_sq, gain, queries, kc, vc, near, far)


def stats_of(ref, heads):
    stats = ref[heads * HD :, :].astype(F32)
    return stats[:heads] + stats[heads : 2 * heads] + stats[2 * heads : 3 * heads]


def merge_kernel(heads, guarded, *refs):
    own, got, out_ref = refs[-3:]
    own_lse, got_lse = stats_of(own, heads), stats_of(got, heads)
    if guarded:
        got_lse = jnp.where(refs[0][0] == 1, got_lse, F32(OUT))
    top = jnp.maximum(own_lse, got_lse)
    own_w, got_w = jnp.exp2(own_lse - top), jnp.exp2(got_lse - top)
    mass = own_w + got_w
    share = 1.0 / mass
    own_w, got_w = own_w * share, got_w * share
    for h in range(heads):
        at = slice(h * HD, (h + 1) * HD)
        mixed = own[at, :].astype(F32) * own_w[h : h + 1] + got[at, :].astype(F32) * got_w[h : h + 1]
        out_ref[at, :] = mixed.astype(BF16)
    out_ref[heads * HD :, :] = split(top + jnp.log2(mass))


def merge(heads, take, own, got):
    guard = [] if take is None else [take.astype(jnp.int32)[None]]
    return pl.pallas_call(
        functools.partial(merge_kernel, heads, bool(guard)),
        out_shape=jax.ShapeDtypeStruct(own.shape, BF16),
        in_specs=[pl.BlockSpec(memory_space=pltpu.SMEM)] * len(guard) + [vmem()] * 2,
        out_specs=vmem(),
        cost_estimate=pl.CostEstimate(
            flops=4 * own.size, bytes_accessed=6 * own.size, transcendentals=0
        ),
        compiler_params=pltpu.CompilerParams(vmem_limit_bytes=4 << 20),
        name="merge",
    )(*guard, own, got)


def local(
    n_slab, n_head, n_seq,
    queries, query_gain, cache_keys, cache_values, finished_keys, finished_values,
    new_keys, new_values, out_weight, time_weight, owner, step,
):
    queries, cache_keys, cache_values, finished_keys, finished_values, new_keys, new_values = in_hbm(
        queries, cache_keys, cache_values, finished_keys, finished_values, new_keys, new_values
    )
    heads = queries.shape[1] // HD
    width = queries.shape[1] * n_head
    slab = lax.axis_index("slab")

    own_sq, near = prepare(queries, finished_keys, new_keys, finished_values, new_values)
    if n_head == 2:
        far_sq = lax.ppermute(own_sq, "head", [(0, 1), (1, 0)])
    else:
        far_sq = lax.psum(own_sq, "head")
        own_sq = jnp.zeros_like(own_sq)
    far = lax.ppermute(near, "seq", [(0, 1), (1, 0)])
    is_owner = (slab == owner).astype(jnp.int32)
    gain = query_gain[None, :]
    gain, near, far = in_hbm(gain, near, far)

    sizes = chunk_sizes(heads)
    starts = [sum(sizes[:c]) for c in range(len(sizes))]
    count = len(sizes)
    side = n_slab // 2
    outer = functools.reduce(jnp.logical_or, [(slab < side - 1), (slab > side)])
    inward = [[(j, j + 1), (n_slab - 1 - j, n_slab - 2 - j)] for j in range(side - 1)]
    outward = [[(b, a) for a, b in pairs] for pairs in inward]
    own, got_in, folded, crossed, total, final = {}, {}, {}, {}, {}, {}
    last = []

    def run(value):
        last[:] = [value]
        return value

    def attention(c):
        flag = in_order(is_owner, *last)
        own[c] = run(
            attend(
                starts[c], sizes[c], width, flag, queries, gain, own_sq,
                far_sq, cache_keys, cache_values, near, far,
            )
        )

    def send_in(c):
        sent = own[c]
        for j in range(side - 2):
            got = lax.ppermute(sent, "slab", inward[j])
            take = (slab == j + 1) | (slab == n_slab - 2 - j)
            sent = merge(sizes[c], take, sent, got)
        own[c] = sent
        got_in[c] = lax.ppermute(sent, "slab", inward[side - 2]) if side > 1 else sent

    def fold(c):
        take = ((slab == side - 1) | (slab == side)) if side != 2 else None
        got = in_order(got_in[c], *last)
        folded[c] = run(merge(sizes[c], take, own[c], got))
        crossed[c] = lax.ppermute(folded[c], "slab", [(side - 1, side), (side, side - 1)])

    def cross(c):
        got = in_order(crossed[c], *last)
        total[c] = run(merge(sizes[c], None, folded[c], got))

    def send_out(c):
        attended = total[c][: sizes[c] * HD]
        for j in range(side - 2, -1, -1):
            got = lax.ppermute(attended, "slab", outward[j])
            attended = jnp.where((slab == j) | (slab == n_slab - 1 - j), got, attended)
        final[c] = attended

    def send_both(c):
        if side != 2 or sizes[c] != sizes[-1]:
            send_in(count - 1)
            send_out(c)
            return
        sent = run(jnp.where(outer, own[count - 1], total[c]))
        got = lax.ppermute(sent, "slab", inward[0] + outward[0])
        got_in[count - 1] = got
        final[c] = jnp.where(outer, got, sent)[: sizes[c] * HD]

    steps = {"A": attention, "I": send_in, "F": fold, "C": cross, "O": send_out, "X": send_both}
    for kind, c in order_of(count):
        steps[kind](c)
    projected = None
    for first, stop in ((0, count - 1), (count - 1, count)):
        attended = jnp.concatenate([final[c] for c in range(first, stop)], axis=0)
        if projected is not None:
            attended = in_order(attended, projected)
        at = starts[first] * HD
        term = lax.dot_general(
            attended, out_weight[at : at + attended.shape[0]], TN, preferred_element_type=F32
        )
        projected = term if projected is None else projected + term

    half = time_weight.shape[0] // 2
    frequency = jnp.exp(-jnp.log(10000.0) * jnp.arange(half, dtype=F32) / half)
    phases = step[0].astype(F32) * frequency
    embedding = jnp.concatenate([jnp.cos(phases), jnp.sin(phases)])
    time_gate = 1.0 + jnp.dot(embedding, time_weight, precision=lax.Precision.HIGHEST)

    cols = time_weight.shape[1]
    if n_head == 2:
        me = lax.axis_index("head")
        left, right = projected[:, :cols], projected[:, cols:]
        kept = jnp.where(me == 0, left, right)
        sent = jnp.where(me == 0, right, left).astype(BF16)
        summed = kept + lax.ppermute(sent, "head", [(0, 1), (1, 0)]).astype(F32)
    else:
        summed = lax.psum_scatter(projected, "head", scatter_dimension=1, tiled=True)
    return (time_gate * summed).astype(BF16)


def solution(mesh):
    in_specs = (
        P(("grp", "seq"), "head"),
        P("head"),
        P(("grp", "slab"), "head"),
        P(("grp", "slab"), "head"),
        P(("grp", "slab", "seq"), "head"),
        P(("grp", "slab", "seq"), "head"),
        P(("grp", "slab", "seq"), "head"),
        P(("grp", "slab", "seq"), "head"),
        P("head", "slab"),
        P(None, ("slab", "head")),
        P("grp"),
        P("grp"),
    )
    out_specs = P(("grp", "seq"), ("slab", "head"))

    def body(*arrays):
        return local(*sizes, *arrays)

    sizes = mesh.shape["slab"], mesh.shape["head"], mesh.shape["seq"]
    return jax.shard_map(body, mesh=mesh, in_specs=in_specs, out_specs=out_specs, check_vma=False)
```

```python
import functools

import jax
import jax.numpy as jnp
from jax import lax
from jax.experimental import pallas as pl
from jax.experimental.pallas import tpu as pltpu
from jax.sharding import PartitionSpec as P


HD = 128
EPSILON = 1e-06
LOG2E = 1.4426950408889634
OUT = -1e30
F32 = jnp.float32
BF16 = jnp.bfloat16
STATS = 16


def chunk_sizes(heads):
    count = -(-heads // 4) if heads > 4 else 2
    return [heads // count + (c < heads % count) for c in range(count)]


def order_of(sizes):
    count = len(sizes)
    if count < 3:
        steps = [(kind, c) for c in range(count) for kind in "AI"]
        steps += [("F", c) for c in range(count)]
        return steps + [(kind, c) for c in range(count) for kind in "CO"]
    steps = [(kind, c) for c in range(3) for kind in "AI"] + [("F", 0)]
    for c in range(3, count):
        steps += [("A", c), ("F", c - 2), ("C", c - 3)]
        steps += [("X", c)] if sizes[c] == sizes[c - 3] else [("I", c), ("O", c - 3)]
    for c in range(max(count - 3, 0), count):
        if c + 1 < count:
            steps += [("F", c + 1)]
        steps += [("C", c), ("O", c)]
    return steps


def in_order(value, *earlier):
    return lax.optimization_barrier((value, *earlier))[0]


def vmem():
    return pl.BlockSpec(memory_space=pltpu.VMEM)


def hbm():
    return pl.BlockSpec(memory_space=pltpu.HBM)


def anywhere():
    return pl.BlockSpec(memory_space=pl.ANY)


def in_hbm(*arrays):
    return [pltpu.with_memory_space_constraint(array, pltpu.HBM) for array in arrays]


def prepare_kernel(q_hbm, fk, nk, fv, nv, squares_ref, near_ref, q_ref, sems):
    rows = fk.shape[0]
    heads = q_ref.shape[1] // HD
    pieces = [slice(c * 5 * HD, min((c + 1) * 5, heads) * HD) for c in range(-(-heads // 5))]
    loads = [
        pltpu.make_async_copy(q_hbm.at[:, piece], q_ref.at[:, piece], sems.at[n + 4])
        for n, piece in enumerate(pieces)
    ]
    copies = [
        pltpu.make_async_copy(src, near_ref.at[pl.ds(n * rows, rows), :], sems.at[n])
        for n, src in enumerate((fk, nk, fv, nv))
    ]
    for copy in loads + copies:
        copy.start()
    total = None
    for h in range(heads):
        if h % 5 == 0:
            loads[h // 5].wait()
        block = q_ref[:, h * HD : (h + 1) * HD].astype(F32)
        term = block * block
        total = term if total is None else total + term
    row = jnp.sum(total.T, axis=0, keepdims=True)
    squares_ref[...] = jnp.broadcast_to(row, squares_ref.shape)
    for copy in copies:
        copy.wait()


def prepare(queries, fk, nk, fv, nv):
    rows = queries.shape[0]
    return pl.pallas_call(
        prepare_kernel,
        out_shape=(
            jax.ShapeDtypeStruct((8, rows), F32),
            jax.ShapeDtypeStruct((4 * fk.shape[0], fk.shape[1]), BF16),
        ),
        in_specs=[hbm()] * 5,
        out_specs=(vmem(), vmem()),
        scratch_shapes=[pltpu.VMEM(queries.shape, BF16), pltpu.SemaphoreType.DMA((4 + -(-queries.shape[1] // (5 * HD)),))],
        cost_estimate=pl.CostEstimate(
            flops=2 * queries.size, bytes_accessed=8 * queries.size, transcendentals=0
        ),
        compiler_params=pltpu.CompilerParams(vmem_limit_bytes=8 << 20),
        name="prepare",
    )(queries, fk, nk, fv, nv)


NT = (((1,), (1,)), ((), ()))
TN = (((0,), (0,)), ((), ()))


def tiles_of(keys, cached, size=256):
    tiles, at = [], 0
    for end in (cached, keys):
        while at < end:
            step = min(size, end - at)
            tiles.append((at, step, end == cached))
            at += step
    return tiles


def by_eight(op, array):
    return op(array.reshape(array.shape[0] // 8, 8, array.shape[1]), axis=0)


def attend_kernel(
    start, heads, width, owner_ref, own_sq, far_sq, gain_hbm, q_hbm, kc_hbm, vc_hbm, near_hbm,
    far_hbm, out_ref, lse_s, s_a, s_b, p_a, p_b, gain_ref, q_ref, k_ref, v_ref, sems,
):
    half = near_hbm.shape[0] // 2
    cached, keys = kc_hbm.shape[0], k_ref.shape[0]
    scale = LOG2E / HD**0.5
    moves = [
        (gain_hbm, 0, gain_hbm.shape[0], gain_ref, 0),
        (q_hbm, 0, q_hbm.shape[0], q_ref, 0),
        (kc_hbm, 0, cached, k_ref, 0),
        (near_hbm, 0, half, k_ref, cached),
        (far_hbm, 0, half, k_ref, cached + half),
        (vc_hbm, 0, cached, v_ref, 0),
        (near_hbm, half, half, v_ref, cached),
        (far_hbm, half, half, v_ref, cached + half),
    ]
    groups = [(0, 1), (1, heads)] if heads > 1 else [(0, 1)]
    copies = []
    for g, (low, high) in enumerate(groups):
        here = slice(low * HD, high * HD)
        there = slice((start + low) * HD, (start + high) * HD)
        copies.append(
            [
                pltpu.make_async_copy(
                    src.at[at : at + size, there], dst.at[to : to + size, here], sems.at[g, n]
                )
                for n, (src, at, size, dst, to) in enumerate(moves)
            ]
        )
        for copy in copies[g]:
            copy.start()
    total = own_sq[0:1, :] + far_sq[0:1, :]
    inverse = lax.rsqrt(total / width + EPSILON)
    inverse = jnp.broadcast_to(inverse, (HD, inverse.shape[1])).T
    penalty = jnp.where(owner_ref[0] == 1, F32(OUT), F32(0.0))
    s_refs, p_refs = (s_a, s_b), (p_a, p_b)
    tiles = tiles_of(keys, cached)
    bases, masses = {}, {}
    for t in range(heads + 2):
        to_score, to_soften, to_gather = t, t - 1, t - 2
        scoring, softening, gathering = t < heads, 0 <= t - 1 < heads, t - 2 >= 0
        if t < len(groups):
            for copy in copies[t]:
                copy.wait()
        if scoring:
            cols = slice(to_score * HD, (to_score + 1) * HD)
            normed = (q_ref[:, cols].astype(F32) * inverse * gain_ref[:, cols]).astype(BF16)
            top = None
        value, mass = None, None
        for at, size, masked in tiles:
            span = slice(at, at + size)
            if gathering:
                part = lax.dot_general(
                    v_ref[span, to_gather * HD : (to_gather + 1) * HD],
                    p_refs[to_gather % 2][span, :],
                    TN,
                    preferred_element_type=F32,
                )
                value = part if value is None else value + part
            if scoring:
                scores = lax.dot_general(k_ref[span, cols], normed, NT, preferred_element_type=F32)
                s_refs[to_score % 2][span, :] = scores
                most = by_eight(jnp.max, scores)
                if masked:
                    most = most + penalty
                top = most if top is None else jnp.maximum(top, most)
            if softening:
                base = bases[to_soften]
                shift = base - penalty if masked else base
                raw = jnp.exp2(s_refs[to_soften % 2][span, :] * scale - shift)
                p_refs[to_soften % 2][span, :] = raw.astype(BF16)
                sums = by_eight(jnp.sum, raw)
                mass = sums if mass is None else mass + sums
        if gathering:
            at = slice(to_gather * HD, (to_gather + 1) * HD)
            out_ref[at, :] = (value * (1.0 / masses[to_gather])).astype(BF16)
        if softening:
            mass = jnp.sum(mass, axis=0, keepdims=True)
            masses[to_soften] = mass
            lse_s[to_soften : to_soften + 1, :] = bases[to_soften] + jnp.log2(mass)
        if scoring:
            bases[to_score] = jnp.max(top, axis=0, keepdims=True) * scale
    out_ref[heads * HD :, :] = split(lse_s[0:heads, :])


def split(lse):
    high = lse.astype(BF16).astype(F32)
    rest = lse - high
    mid = rest.astype(BF16).astype(F32)
    low = rest - mid
    pad = jnp.zeros((STATS - 3 * lse.shape[0], lse.shape[1]), F32)
    return jnp.concatenate([high, mid, low, pad], axis=0).astype(BF16)


def attend(start, heads, width, is_owner, queries, gain, own_sq, far_sq, kc, vc, near, far):
    rows = queries.shape[0]
    keys = kc.shape[0] + near.shape[0]
    wide = heads * HD
    return pl.pallas_call(
        functools.partial(attend_kernel, start, heads, width),
        out_shape=jax.ShapeDtypeStruct((wide + STATS, rows), BF16),
        in_specs=[pl.BlockSpec(memory_space=pltpu.SMEM)] + [vmem()] * 2 + [hbm()] * 5 + [anywhere()],
        out_specs=vmem(),
        scratch_shapes=[pltpu.VMEM((8, rows), F32)]
        + [pltpu.VMEM((keys, rows), F32)] * 2
        + [pltpu.VMEM((keys, rows), BF16)] * 2
        + [pltpu.VMEM((1, wide), F32), pltpu.VMEM((rows, wide), BF16)]
        + [pltpu.VMEM((keys, wide), BF16)] * 2
        + [pltpu.SemaphoreType.DMA((2, 8))],
        cost_estimate=pl.CostEstimate(
            flops=16 * heads * rows * keys * HD,
            bytes_accessed=4 * heads * keys * HD,
            transcendentals=heads * rows * keys,
        ),
        compiler_params=pltpu.CompilerParams(vmem_limit_bytes=12 << 20),
        name="attend",
    )(is_owner, own_sq, far_sq, gain, queries, kc, vc, near, far)


def stats_of(ref, heads):
    stats = ref[heads * HD :, :].astype(F32)
    return stats[:heads] + stats[heads : 2 * heads] + stats[2 * heads : 3 * heads]


def merge_kernel(heads, guarded, *refs):
    own, got, out_ref = refs[-3:]
    own_lse, got_lse = stats_of(own, heads), stats_of(got, heads)
    if guarded:
        got_lse = jnp.where(refs[0][0] == 1, got_lse, F32(OUT))
    top = jnp.maximum(own_lse, got_lse)
    own_w, got_w = jnp.exp2(own_lse - top), jnp.exp2(got_lse - top)
    mass = own_w + got_w
    share = 1.0 / mass
    own_w, got_w = own_w * share, got_w * share
    for h in range(heads):
        at = slice(h * HD, (h + 1) * HD)
        mixed = own[at, :].astype(F32) * own_w[h : h + 1] + got[at, :].astype(F32) * got_w[h : h + 1]
        out_ref[at, :] = mixed.astype(BF16)
    out_ref[heads * HD :, :] = split(top + jnp.log2(mass))


def merge(heads, take, own, got):
    guard = [] if take is None else [take.astype(jnp.int32)[None]]
    return pl.pallas_call(
        functools.partial(merge_kernel, heads, bool(guard)),
        out_shape=jax.ShapeDtypeStruct(own.shape, BF16),
        in_specs=[pl.BlockSpec(memory_space=pltpu.SMEM)] * len(guard) + [vmem()] * 2,
        out_specs=vmem(),
        cost_estimate=pl.CostEstimate(
            flops=4 * own.size, bytes_accessed=6 * own.size, transcendentals=0
        ),
        compiler_params=pltpu.CompilerParams(vmem_limit_bytes=4 << 20),
        name="merge",
    )(*guard, own, got)


def project_kernel(parts, attended_ref, weight_hbm, sum_ref, later_ref, turned, weight, sems):
    depth, cols = attended_ref.shape[0], sum_ref.shape[1]
    step = depth // parts
    copies = [
        pltpu.make_async_copy(
            weight_hbm.at[pl.ds(n * step, step), :], weight.at[pl.ds(n * step, step), :], sems.at[n]
        )
        for n in range(parts)
    ]
    copies.append(
        pltpu.make_async_copy(
            weight_hbm.at[pl.ds(depth, later_ref.shape[0]), :], later_ref, sems.at[parts]
        )
    )
    for copy in copies:
        copy.start()
    turned[...] = attended_ref[...].T
    for n in range(parts):
        copies[n].wait()
        span = slice(n * step, (n + 1) * step)
        for low in range(0, cols, 256):
            tile = slice(low, min(low + 256, cols))
            term = jnp.dot(turned[:, span], weight[span, tile], preferred_element_type=F32)
            sum_ref[:, tile] = term if n == 0 else sum_ref[:, tile] + term
    copies[parts].wait()


def project(parts, attended, weight):
    depth, rows = attended.shape
    cols = weight.shape[1]
    return pl.pallas_call(
        functools.partial(project_kernel, parts),
        out_shape=(
            jax.ShapeDtypeStruct((rows, cols), F32),
            jax.ShapeDtypeStruct((weight.shape[0] - depth, cols), BF16),
        ),
        in_specs=[vmem(), hbm()],
        out_specs=(vmem(), vmem()),
        scratch_shapes=[
            pltpu.VMEM((rows, depth), BF16),
            pltpu.VMEM((depth, cols), BF16),
            pltpu.SemaphoreType.DMA((parts + 1,)),
        ],
        cost_estimate=pl.CostEstimate(
            flops=2 * depth * rows * cols, bytes_accessed=2 * weight.size, transcendentals=0
        ),
        compiler_params=pltpu.CompilerParams(vmem_limit_bytes=16 << 20),
        name="project",
    )(attended, weight)


def finish_kernel(attended_ref, weight_ref, sum_ref, out_ref):
    turned = attended_ref[...].T
    for low in range(0, out_ref.shape[1], 256):
        tile = slice(low, min(low + 256, out_ref.shape[1]))
        term = jnp.dot(turned, weight_ref[:, tile], preferred_element_type=F32)
        out_ref[:, tile] = sum_ref[:, tile] + term


def finish(attended, weight, summed):
    return pl.pallas_call(
        finish_kernel,
        out_shape=jax.ShapeDtypeStruct(summed.shape, F32),
        in_specs=[vmem()] * 3,
        out_specs=vmem(),
        cost_estimate=pl.CostEstimate(
            flops=2 * attended.size * weight.shape[1],
            bytes_accessed=2 * weight.size,
            transcendentals=0,
        ),
        compiler_params=pltpu.CompilerParams(vmem_limit_bytes=12 << 20),
        name="finish",
    )(attended, weight, summed)


def local(
    n_slab, n_head, n_seq,
    queries, query_gain, cache_keys, cache_values, finished_keys, finished_values,
    new_keys, new_values, out_weight, time_weight, owner, step,
):
    queries, cache_keys, cache_values, finished_keys, finished_values, new_keys, new_values = in_hbm(
        queries, cache_keys, cache_values, finished_keys, finished_values, new_keys, new_values
    )
    (out_weight,) = in_hbm(out_weight)
    heads = queries.shape[1] // HD
    width = queries.shape[1] * n_head
    slab = lax.axis_index("slab")

    own_sq, near = prepare(queries, finished_keys, new_keys, finished_values, new_values)
    if n_head == 2:
        far_sq = lax.ppermute(own_sq, "head", [(0, 1), (1, 0)])
    else:
        far_sq = lax.psum(own_sq, "head")
        own_sq = jnp.zeros_like(own_sq)
    far = lax.ppermute(near, "seq", [(0, 1), (1, 0)])
    is_owner = (slab == owner).astype(jnp.int32)
    gain = query_gain[None, :]
    first_far = far
    gain, near, far = in_hbm(gain, near, far)

    sizes = chunk_sizes(heads)
    starts = [sum(sizes[:c]) for c in range(len(sizes))]
    count = len(sizes)
    side = n_slab // 2
    outer = functools.reduce(jnp.logical_or, [(slab < side - 1), (slab > side)])
    inward = [[(j, j + 1), (n_slab - 1 - j, n_slab - 2 - j)] for j in range(side - 1)]
    outward = [[(b, a) for a, b in pairs] for pairs in inward]
    own, got_in, folded, crossed, total, final = {}, {}, {}, {}, {}, {}
    last = []

    def run(value):
        last[:] = [value]
        return value

    def attention(c):
        flag = in_order(is_owner, *last)
        own[c] = run(
            attend(
                starts[c], sizes[c], width, flag, queries, gain, own_sq,
                far_sq, cache_keys, cache_values, near, far if c else first_far,
            )
        )

    def send_in(c):
        sent = own[c]
        for j in range(side - 2):
            got = lax.ppermute(sent, "slab", inward[j])
            take = (slab == j + 1) | (slab == n_slab - 2 - j)
            sent = merge(sizes[c], take, sent, got)
        own[c] = sent
        got_in[c] = lax.ppermute(sent, "slab", inward[side - 2]) if side > 1 else sent

    def fold(c):
        take = ((slab == side - 1) | (slab == side)) if side != 2 else None
        got = in_order(got_in[c], *last)
        folded[c] = run(merge(sizes[c], take, own[c], got))
        crossed[c] = lax.ppermute(folded[c], "slab", [(side - 1, side), (side, side - 1)])

    def cross(c):
        got = in_order(crossed[c], *last)
        total[c] = run(merge(sizes[c], None, folded[c], got))

    def send_out(c):
        attended = total[c][: sizes[c] * HD]
        for j in range(side - 2, -1, -1):
            got = lax.ppermute(attended, "slab", outward[j])
            attended = jnp.where((slab == j) | (slab == n_slab - 1 - j), got, attended)
        final[c] = attended

    def send_both(c):
        if side != 2:
            send_in(c)
            send_out(c - 3)
            return
        sent = run(jnp.where(outer, own[c], total[c - 3]))
        got = lax.ppermute(sent, "slab", inward[0] + outward[0])
        got_in[c] = got
        final[c - 3] = jnp.where(outer, got, sent)[: sizes[c - 3] * HD]

    steps = {"A": attention, "I": send_in, "F": fold, "C": cross, "O": send_out, "X": send_both}
    for kind, c in order_of(sizes):
        steps[kind](c)
    early = jnp.concatenate([final[c] for c in range(count - 1)], axis=0)
    projected, later = project(count - 1, in_order(early, *last), out_weight)
    projected = finish(in_order(final[count - 1], projected), later, projected)

    half = time_weight.shape[0] // 2
    frequency = jnp.exp(-jnp.log(10000.0) * jnp.arange(half, dtype=F32) / half)
    phases = step[0].astype(F32) * frequency
    embedding = jnp.concatenate([jnp.cos(phases), jnp.sin(phases)])
    time_gate = 1.0 + jnp.dot(embedding, time_weight, precision=lax.Precision.HIGHEST)

    cols = time_weight.shape[1]
    if n_head == 2:
        me = lax.axis_index("head")
        left, right = projected[:, :cols], projected[:, cols:]
        kept = jnp.where(me == 0, left, right)
        sent = jnp.where(me == 0, right, left).astype(BF16)
        summed = kept + lax.ppermute(sent, "head", [(0, 1), (1, 0)]).astype(F32)
    else:
        summed = lax.psum_scatter(projected, "head", scatter_dimension=1, tiled=True)
    return (time_gate * summed).astype(BF16)


def solution(mesh):
    in_specs = (
        P(("grp", "seq"), "head"),
        P("head"),
        P(("grp", "slab"), "head"),
        P(("grp", "slab"), "head"),
        P(("grp", "slab", "seq"), "head"),
        P(("grp", "slab", "seq"), "head"),
        P(("grp", "slab", "seq"), "head"),
        P(("grp", "slab", "seq"), "head"),
        P("head", "slab"),
        P(None, ("slab", "head")),
        P("grp"),
        P("grp"),
    )
    out_specs = P(("grp", "seq"), ("slab", "head"))

    def body(*arrays):
        return local(*sizes, *arrays)

    sizes = mesh.shape["slab"], mesh.shape["head"], mesh.shape["seq"]
    return jax.shard_map(body, mesh=mesh, in_specs=in_specs, out_specs=out_specs, check_vma=False)
```

```python
import functools

import jax
import jax.numpy as jnp
from jax import lax
from jax.experimental import pallas as pl
from jax.experimental.pallas import tpu as pltpu
from jax.sharding import PartitionSpec as P


HD = 128
EPSILON = 1e-06
LOG2E = 1.4426950408889634
OUT = -1e30
F32 = jnp.float32
BF16 = jnp.bfloat16
STATS = 16


def chunk_sizes(heads):
    count = -(-heads // 4) if heads > 4 else 2
    sizes = [heads // count + (c < heads % count) for c in range(count)]
    if count > 3:
        sizes[0], sizes[1] = sizes[0] - 1, sizes[1] + 1
    return sizes


def order_of(sizes):
    count = len(sizes)
    if count < 3:
        steps = [(kind, c) for c in range(count) for kind in "AI"]
        steps += [("F", c) for c in range(count)]
        return steps + [(kind, c) for c in range(count) for kind in "CO"]
    steps = [(kind, c) for c in range(3) for kind in "AI"] + [("F", 0)]
    for c in range(3, count):
        steps += [("A", c), ("F", c - 2), ("C", c - 3)]
        steps += [("X", c)]
    for c in range(max(count - 3, 0), count):
        if c + 1 < count:
            steps += [("F", c + 1)]
        steps += [("C", c), ("O", c)]
    return steps


def in_order(value, *earlier):
    return lax.optimization_barrier((value, *earlier))[0]


def vmem():
    return pl.BlockSpec(memory_space=pltpu.VMEM)


def hbm():
    return pl.BlockSpec(memory_space=pltpu.HBM)


def anywhere():
    return pl.BlockSpec(memory_space=pl.ANY)


def in_hbm(*arrays):
    return [pltpu.with_memory_space_constraint(array, pltpu.HBM) for array in arrays]


def prepare_kernel(q_hbm, fk, nk, fv, nv, squares_ref, near_ref, q_ref, sems):
    rows = fk.shape[0]
    heads = q_ref.shape[1] // HD
    pieces = [slice(c * 5 * HD, min((c + 1) * 5, heads) * HD) for c in range(-(-heads // 5))]
    loads = [
        pltpu.make_async_copy(q_hbm.at[:, piece], q_ref.at[:, piece], sems.at[n + 4])
        for n, piece in enumerate(pieces)
    ]
    copies = [
        pltpu.make_async_copy(src, near_ref.at[pl.ds(n * rows, rows), :], sems.at[n])
        for n, src in enumerate((fk, nk, fv, nv))
    ]
    for copy in loads + copies:
        copy.start()
    total = None
    for h in range(heads):
        if h % 5 == 0:
            loads[h // 5].wait()
        block = q_ref[:, h * HD : (h + 1) * HD].astype(F32)
        term = block * block
        total = term if total is None else total + term
    row = jnp.sum(total.T, axis=0, keepdims=True)
    squares_ref[...] = jnp.broadcast_to(row, squares_ref.shape)
    for copy in copies:
        copy.wait()


def prepare(queries, fk, nk, fv, nv):
    rows = queries.shape[0]
    return pl.pallas_call(
        prepare_kernel,
        out_shape=(
            jax.ShapeDtypeStruct((8, rows), F32),
            jax.ShapeDtypeStruct((4 * fk.shape[0], fk.shape[1]), BF16),
        ),
        in_specs=[hbm()] * 5,
        out_specs=(vmem(), vmem()),
        scratch_shapes=[pltpu.VMEM(queries.shape, BF16), pltpu.SemaphoreType.DMA((4 + -(-queries.shape[1] // (5 * HD)),))],
        cost_estimate=pl.CostEstimate(
            flops=2 * queries.size, bytes_accessed=8 * queries.size, transcendentals=0
        ),
        compiler_params=pltpu.CompilerParams(vmem_limit_bytes=8 << 20),
        name="prepare",
    )(queries, fk, nk, fv, nv)


NT = (((1,), (1,)), ((), ()))
TN = (((0,), (0,)), ((), ()))


def tiles_of(keys, cached, size=256):
    tiles, at = [], 0
    for end in (cached, keys):
        while at < end:
            step = min(size, end - at)
            tiles.append((at, step, end == cached))
            at += step
    return tiles


def by_eight(op, array):
    return op(array.reshape(array.shape[0] // 8, 8, array.shape[1]), axis=0)


def attend_kernel(
    start, heads, width, owner_ref, own_sq, far_sq, gain_hbm, q_hbm, kc_hbm, vc_hbm, near_hbm,
    far_hbm, out_ref, lse_s, s_a, s_b, p_a, p_b, gain_ref, q_ref, k_ref, v_ref, sems,
):
    half = near_hbm.shape[0] // 2
    cached, keys = kc_hbm.shape[0], k_ref.shape[0]
    scale = LOG2E / HD**0.5
    moves = [
        (gain_hbm, 0, gain_hbm.shape[0], gain_ref, 0),
        (q_hbm, 0, q_hbm.shape[0], q_ref, 0),
        (kc_hbm, 0, cached, k_ref, 0),
        (near_hbm, 0, half, k_ref, cached),
        (far_hbm, 0, half, k_ref, cached + half),
        (vc_hbm, 0, cached, v_ref, 0),
        (near_hbm, half, half, v_ref, cached),
        (far_hbm, half, half, v_ref, cached + half),
    ]
    groups = [(0, 1), (1, heads)] if heads > 1 else [(0, 1)]
    copies = []
    for g, (low, high) in enumerate(groups):
        here = slice(low * HD, high * HD)
        there = slice((start + low) * HD, (start + high) * HD)
        copies.append(
            [
                pltpu.make_async_copy(
                    src.at[at : at + size, there], dst.at[to : to + size, here], sems.at[g, n]
                )
                for n, (src, at, size, dst, to) in enumerate(moves)
            ]
        )
        for copy in copies[g]:
            copy.start()
    total = own_sq[0:1, :] + far_sq[0:1, :]
    inverse = lax.rsqrt(total / width + EPSILON)
    inverse = jnp.broadcast_to(inverse, (HD, inverse.shape[1])).T
    penalty = jnp.where(owner_ref[0] == 1, F32(OUT), F32(0.0))
    s_refs, p_refs = (s_a, s_b), (p_a, p_b)
    tiles = tiles_of(keys, cached)
    bases, masses = {}, {}
    for t in range(heads + 2):
        to_score, to_soften, to_gather = t, t - 1, t - 2
        scoring, softening, gathering = t < heads, 0 <= t - 1 < heads, t - 2 >= 0
        if t < len(groups):
            for copy in copies[t]:
                copy.wait()
        if scoring:
            cols = slice(to_score * HD, (to_score + 1) * HD)
            normed = (q_ref[:, cols].astype(F32) * inverse * gain_ref[:, cols]).astype(BF16)
            top = None
        value, mass = None, None
        for at, size, masked in tiles:
            span = slice(at, at + size)
            if gathering:
                part = lax.dot_general(
                    v_ref[span, to_gather * HD : (to_gather + 1) * HD],
                    p_refs[to_gather % 2][span, :],
                    TN,
                    preferred_element_type=F32,
                )
                value = part if value is None else value + part
            if scoring:
                scores = lax.dot_general(k_ref[span, cols], normed, NT, preferred_element_type=F32)
                s_refs[to_score % 2][span, :] = scores
                most = by_eight(jnp.max, scores)
                if masked:
                    most = most + penalty
                top = most if top is None else jnp.maximum(top, most)
            if softening:
                base = bases[to_soften]
                shift = base - penalty if masked else base
                raw = jnp.exp2(s_refs[to_soften % 2][span, :] * scale - shift)
                p_refs[to_soften % 2][span, :] = raw.astype(BF16)
                sums = by_eight(jnp.sum, raw)
                mass = sums if mass is None else mass + sums
        if gathering:
            at = slice(to_gather * HD, (to_gather + 1) * HD)
            out_ref[at, :] = (value * (1.0 / masses[to_gather])).astype(BF16)
        if softening:
            mass = jnp.sum(mass, axis=0, keepdims=True)
            masses[to_soften] = mass
            lse_s[to_soften : to_soften + 1, :] = bases[to_soften] + jnp.log2(mass)
        if scoring:
            bases[to_score] = jnp.max(top, axis=0, keepdims=True) * scale
    out_ref[heads * HD :, :] = split(lse_s[0:heads, :])


def split(lse):
    high = lse.astype(BF16).astype(F32)
    rest = lse - high
    mid = rest.astype(BF16).astype(F32)
    low = rest - mid
    pad = jnp.zeros((STATS - 3 * lse.shape[0], lse.shape[1]), F32)
    return jnp.concatenate([high, mid, low, pad], axis=0).astype(BF16)


def attend(start, heads, width, is_owner, queries, gain, own_sq, far_sq, kc, vc, near, far):
    rows = queries.shape[0]
    keys = kc.shape[0] + near.shape[0]
    wide = heads * HD
    return pl.pallas_call(
        functools.partial(attend_kernel, start, heads, width),
        out_shape=jax.ShapeDtypeStruct((wide + STATS, rows), BF16),
        in_specs=[pl.BlockSpec(memory_space=pltpu.SMEM)] + [vmem()] * 2 + [hbm()] * 5 + [anywhere()],
        out_specs=vmem(),
        scratch_shapes=[pltpu.VMEM((8, rows), F32)]
        + [pltpu.VMEM((keys, rows), F32)] * 2
        + [pltpu.VMEM((keys, rows), BF16)] * 2
        + [pltpu.VMEM((1, wide), F32), pltpu.VMEM((rows, wide), BF16)]
        + [pltpu.VMEM((keys, wide), BF16)] * 2
        + [pltpu.SemaphoreType.DMA((2, 8))],
        cost_estimate=pl.CostEstimate(
            flops=16 * heads * rows * keys * HD,
            bytes_accessed=4 * heads * keys * HD,
            transcendentals=heads * rows * keys,
        ),
        compiler_params=pltpu.CompilerParams(vmem_limit_bytes=12 << 20),
        name="attend",
    )(is_owner, own_sq, far_sq, gain, queries, kc, vc, near, far)


def stats_of(ref, heads):
    stats = ref[heads * HD :, :].astype(F32)
    return stats[:heads] + stats[heads : 2 * heads] + stats[2 * heads : 3 * heads]


def merge_kernel(heads, guarded, *refs):
    own, got, out_ref = refs[-3:]
    own_lse, got_lse = stats_of(own, heads), stats_of(got, heads)
    if guarded:
        got_lse = jnp.where(refs[0][0] == 1, got_lse, F32(OUT))
    top = jnp.maximum(own_lse, got_lse)
    own_w, got_w = jnp.exp2(own_lse - top), jnp.exp2(got_lse - top)
    mass = own_w + got_w
    share = 1.0 / mass
    own_w, got_w = own_w * share, got_w * share
    for h in range(heads):
        at = slice(h * HD, (h + 1) * HD)
        mixed = own[at, :].astype(F32) * own_w[h : h + 1] + got[at, :].astype(F32) * got_w[h : h + 1]
        out_ref[at, :] = mixed.astype(BF16)
    out_ref[heads * HD :, :] = split(top + jnp.log2(mass))


def merge(heads, take, own, got):
    guard = [] if take is None else [take.astype(jnp.int32)[None]]
    return pl.pallas_call(
        functools.partial(merge_kernel, heads, bool(guard)),
        out_shape=jax.ShapeDtypeStruct(own.shape, BF16),
        in_specs=[pl.BlockSpec(memory_space=pltpu.SMEM)] * len(guard) + [vmem()] * 2,
        out_specs=vmem(),
        cost_estimate=pl.CostEstimate(
            flops=4 * own.size, bytes_accessed=6 * own.size, transcendentals=0
        ),
        compiler_params=pltpu.CompilerParams(vmem_limit_bytes=4 << 20),
        name="merge",
    )(*guard, own, got)


def project_kernel(bounds, attended_ref, weight_hbm, sum_ref, later_ref, turned, weight, sems):
    depth, cols = attended_ref.shape[0], sum_ref.shape[1]
    parts = len(bounds) - 1
    spans = [slice(low, high) for low, high in zip(bounds[:-1], bounds[1:])]
    copies = [
        pltpu.make_async_copy(weight_hbm.at[span, :], weight.at[span, :], sems.at[n])
        for n, span in enumerate(spans)
    ]
    copies.append(
        pltpu.make_async_copy(
            weight_hbm.at[pl.ds(depth, later_ref.shape[0]), :], later_ref, sems.at[parts]
        )
    )
    for copy in copies:
        copy.start()
    turned[...] = attended_ref[...].T
    for n in range(parts):
        copies[n].wait()
        span = spans[n]
        for low in range(0, cols, 256):
            tile = slice(low, min(low + 256, cols))
            term = jnp.dot(turned[:, span], weight[span, tile], preferred_element_type=F32)
            sum_ref[:, tile] = term if n == 0 else sum_ref[:, tile] + term
    copies[parts].wait()


def project(bounds, attended, weight):
    depth, rows = attended.shape
    cols = weight.shape[1]
    return pl.pallas_call(
        functools.partial(project_kernel, bounds),
        out_shape=(
            jax.ShapeDtypeStruct((rows, cols), F32),
            jax.ShapeDtypeStruct((weight.shape[0] - depth, cols), BF16),
        ),
        in_specs=[vmem(), hbm()],
        out_specs=(vmem(), vmem()),
        scratch_shapes=[
            pltpu.VMEM((rows, depth), BF16),
            pltpu.VMEM((depth, cols), BF16),
            pltpu.SemaphoreType.DMA((len(bounds),)),
        ],
        cost_estimate=pl.CostEstimate(
            flops=2 * depth * rows * cols, bytes_accessed=2 * weight.size, transcendentals=0
        ),
        compiler_params=pltpu.CompilerParams(vmem_limit_bytes=16 << 20),
        name="project",
    )(attended, weight)


def finish_kernel(attended_ref, weight_ref, sum_ref, out_ref):
    turned = attended_ref[...].T
    for low in range(0, out_ref.shape[1], 256):
        tile = slice(low, min(low + 256, out_ref.shape[1]))
        term = jnp.dot(turned, weight_ref[:, tile], preferred_element_type=F32)
        out_ref[:, tile] = sum_ref[:, tile] + term


def finish(attended, weight, summed):
    return pl.pallas_call(
        finish_kernel,
        out_shape=jax.ShapeDtypeStruct(summed.shape, F32),
        in_specs=[vmem()] * 3,
        out_specs=vmem(),
        cost_estimate=pl.CostEstimate(
            flops=2 * attended.size * weight.shape[1],
            bytes_accessed=2 * weight.size,
            transcendentals=0,
        ),
        compiler_params=pltpu.CompilerParams(vmem_limit_bytes=12 << 20),
        name="finish",
    )(attended, weight, summed)


def local(
    n_slab, n_head, n_seq,
    queries, query_gain, cache_keys, cache_values, finished_keys, finished_values,
    new_keys, new_values, out_weight, time_weight, owner, step,
):
    queries, cache_keys, cache_values, finished_keys, finished_values, new_keys, new_values = in_hbm(
        queries, cache_keys, cache_values, finished_keys, finished_values, new_keys, new_values
    )
    (out_weight,) = in_hbm(out_weight)
    heads = queries.shape[1] // HD
    width = queries.shape[1] * n_head
    slab = lax.axis_index("slab")

    own_sq, near = prepare(queries, finished_keys, new_keys, finished_values, new_values)
    if n_head == 2:
        far_sq = lax.ppermute(own_sq, "head", [(0, 1), (1, 0)])
    else:
        far_sq = lax.psum(own_sq, "head")
        own_sq = jnp.zeros_like(own_sq)
    far = lax.ppermute(near, "seq", [(0, 1), (1, 0)])
    is_owner = (slab == owner).astype(jnp.int32)
    gain = query_gain[None, :]
    first_far = far
    gain, near, far = in_hbm(gain, near, far)

    sizes = chunk_sizes(heads)
    starts = [sum(sizes[:c]) for c in range(len(sizes))]
    count = len(sizes)
    side = n_slab // 2
    outer = functools.reduce(jnp.logical_or, [(slab < side - 1), (slab > side)])
    inward = [[(j, j + 1), (n_slab - 1 - j, n_slab - 2 - j)] for j in range(side - 1)]
    outward = [[(b, a) for a, b in pairs] for pairs in inward]
    own, got_in, folded, crossed, total, final = {}, {}, {}, {}, {}, {}
    last = []

    def run(value):
        last[:] = [value]
        return value

    def attention(c):
        flag = in_order(is_owner, *last)
        own[c] = run(
            attend(
                starts[c], sizes[c], width, flag, queries, gain, own_sq,
                far_sq, cache_keys, cache_values, near, far if c else first_far,
            )
        )

    def send_in(c):
        sent = own[c]
        for j in range(side - 2):
            got = lax.ppermute(sent, "slab", inward[j])
            take = (slab == j + 1) | (slab == n_slab - 2 - j)
            sent = merge(sizes[c], take, sent, got)
        own[c] = sent
        got_in[c] = lax.ppermute(sent, "slab", inward[side - 2]) if side > 1 else sent

    def fold(c):
        take = ((slab == side - 1) | (slab == side)) if side != 2 else None
        got = in_order(got_in[c], *last)
        folded[c] = run(merge(sizes[c], take, own[c], got))
        crossed[c] = lax.ppermute(folded[c], "slab", [(side - 1, side), (side, side - 1)])

    def cross(c):
        got = in_order(crossed[c], *last)
        total[c] = run(merge(sizes[c], None, folded[c], got))

    def send_out(c):
        attended = total[c][: sizes[c] * HD]
        for j in range(side - 2, -1, -1):
            got = lax.ppermute(attended, "slab", outward[j])
            attended = jnp.where((slab == j) | (slab == n_slab - 1 - j), got, attended)
        final[c] = attended

    def send_both(c):
        if side != 2:
            send_in(c)
            send_out(c - 3)
            return
        rows = max(own[c].shape[0], total[c - 3].shape[0])
        going, coming = (
            jnp.pad(m, ((0, rows - m.shape[0]), (0, 0))) for m in (own[c], total[c - 3])
        )
        sent = run(jnp.where(outer, going, coming))
        got = lax.ppermute(sent, "slab", inward[0] + outward[0])
        got_in[c] = got[: own[c].shape[0]]
        final[c - 3] = jnp.where(outer, got, sent)[: sizes[c - 3] * HD]

    steps = {"A": attention, "I": send_in, "F": fold, "C": cross, "O": send_out, "X": send_both}
    for kind, c in order_of(sizes):
        steps[kind](c)
    early = jnp.concatenate([final[c] for c in range(count - 1)], axis=0)
    bounds = tuple(start * HD for start in starts)
    projected, later = project(bounds, in_order(early, *last), out_weight)
    projected = finish(in_order(final[count - 1], projected), later, projected)

    half = time_weight.shape[0] // 2
    frequency = jnp.exp(-jnp.log(10000.0) * jnp.arange(half, dtype=F32) / half)
    phases = step[0].astype(F32) * frequency
    embedding = jnp.concatenate([jnp.cos(phases), jnp.sin(phases)])
    time_gate = 1.0 + jnp.dot(embedding, time_weight, precision=lax.Precision.HIGHEST)

    cols = time_weight.shape[1]
    if n_head == 2:
        me = lax.axis_index("head")
        left, right = projected[:, :cols], projected[:, cols:]
        kept = jnp.where(me == 0, left, right)
        sent = jnp.where(me == 0, right, left).astype(BF16)
        summed = kept + lax.ppermute(sent, "head", [(0, 1), (1, 0)]).astype(F32)
    else:
        summed = lax.psum_scatter(projected, "head", scatter_dimension=1, tiled=True)
    return (time_gate * summed).astype(BF16)


def solution(mesh):
    in_specs = (
        P(("grp", "seq"), "head"),
        P("head"),
        P(("grp", "slab"), "head"),
        P(("grp", "slab"), "head"),
        P(("grp", "slab", "seq"), "head"),
        P(("grp", "slab", "seq"), "head"),
        P(("grp", "slab", "seq"), "head"),
        P(("grp", "slab", "seq"), "head"),
        P("head", "slab"),
        P(None, ("slab", "head")),
        P("grp"),
        P("grp"),
    )
    out_specs = P(("grp", "seq"), ("slab", "head"))

    def body(*arrays):
        return local(*sizes, *arrays)

    sizes = mesh.shape["slab"], mesh.shape["head"], mesh.shape["seq"]
    return jax.shard_map(body, mesh=mesh, in_specs=in_specs, out_specs=out_specs, check_vma=False)
```

```python
import functools

import jax
import jax.numpy as jnp
from jax import lax
from jax.experimental import pallas as pl
from jax.experimental.pallas import tpu as pltpu
from jax.sharding import PartitionSpec as P


HD = 128
EPSILON = 1e-06
LOG2E = 1.4426950408889634
OUT = -1e30
F32 = jnp.float32
BF16 = jnp.bfloat16
STATS = 16


def chunk_sizes(heads):
    count = -(-heads // 4) if heads > 4 else 2
    sizes = [heads // count + (c < heads % count) for c in range(count)]
    if count > 3:
        sizes[0], sizes[1] = sizes[0] - 1, sizes[1] + 1
    return sizes


def order_of(sizes):
    count = len(sizes)
    if count < 3:
        steps = [(kind, c) for c in range(count) for kind in "AI"]
        steps += [("F", c) for c in range(count)]
        return steps + [(kind, c) for c in range(count) for kind in "CO"]
    steps = [(kind, c) for c in range(3) for kind in "AI"] + [("F", 0)]
    for c in range(3, count):
        steps += [("A", c), ("F", c - 2), ("C", c - 3)]
        steps += [("X", c)]
    for c in range(max(count - 3, 0), count):
        if c + 1 < count:
            steps += [("F", c + 1)]
        steps += [("C", c), ("O", c)]
    steps += [("P", count - 3)]
    return steps


def in_order(value, *earlier):
    return lax.optimization_barrier((value, *earlier))[0]


def vmem():
    return pl.BlockSpec(memory_space=pltpu.VMEM)


def hbm():
    return pl.BlockSpec(memory_space=pltpu.HBM)


def anywhere():
    return pl.BlockSpec(memory_space=pl.ANY)


def in_hbm(*arrays):
    return [pltpu.with_memory_space_constraint(array, pltpu.HBM) for array in arrays]


def prepare_kernel(q_hbm, fk, nk, fv, nv, squares_ref, near_ref, q_ref, sems):
    rows = fk.shape[0]
    heads = q_ref.shape[1] // HD
    pieces = [slice(c * 5 * HD, min((c + 1) * 5, heads) * HD) for c in range(-(-heads // 5))]
    loads = [
        pltpu.make_async_copy(q_hbm.at[:, piece], q_ref.at[:, piece], sems.at[n + 4])
        for n, piece in enumerate(pieces)
    ]
    copies = [
        pltpu.make_async_copy(src, near_ref.at[pl.ds(n * rows, rows), :], sems.at[n])
        for n, src in enumerate((fk, nk, fv, nv))
    ]
    for copy in loads + copies:
        copy.start()
    total = None
    for h in range(heads):
        if h % 5 == 0:
            loads[h // 5].wait()
        block = q_ref[:, h * HD : (h + 1) * HD].astype(F32)
        term = block * block
        total = term if total is None else total + term
    row = jnp.sum(total.T, axis=0, keepdims=True)
    squares_ref[...] = jnp.broadcast_to(row, squares_ref.shape)
    for copy in copies:
        copy.wait()


def prepare(queries, fk, nk, fv, nv):
    rows = queries.shape[0]
    return pl.pallas_call(
        prepare_kernel,
        out_shape=(
            jax.ShapeDtypeStruct((8, rows), F32),
            jax.ShapeDtypeStruct((4 * fk.shape[0], fk.shape[1]), BF16),
        ),
        in_specs=[hbm()] * 5,
        out_specs=(vmem(), vmem()),
        scratch_shapes=[pltpu.VMEM(queries.shape, BF16), pltpu.SemaphoreType.DMA((4 + -(-queries.shape[1] // (5 * HD)),))],
        cost_estimate=pl.CostEstimate(
            flops=2 * queries.size, bytes_accessed=8 * queries.size, transcendentals=0
        ),
        compiler_params=pltpu.CompilerParams(vmem_limit_bytes=8 << 20),
        name="prepare",
    )(queries, fk, nk, fv, nv)


NT = (((1,), (1,)), ((), ()))
TN = (((0,), (0,)), ((), ()))


def tiles_of(keys, cached, size=256):
    tiles, at = [], 0
    for end in (cached, keys):
        while at < end:
            step = min(size, end - at)
            tiles.append((at, step, end == cached))
            at += step
    return tiles


def by_eight(op, array):
    return op(array.reshape(array.shape[0] // 8, 8, array.shape[1]), axis=0)


def attend_kernel(
    start, heads, width, owner_ref, own_sq, far_sq, gain_hbm, q_hbm, kc_hbm, vc_hbm, near_hbm,
    far_hbm, out_ref, lse_s, s_a, s_b, p_a, p_b, gain_ref, q_ref, k_ref, v_ref, sems,
):
    half = near_hbm.shape[0] // 2
    cached, keys = kc_hbm.shape[0], k_ref.shape[0]
    scale = LOG2E / HD**0.5
    moves = [
        (gain_hbm, 0, gain_hbm.shape[0], gain_ref, 0),
        (q_hbm, 0, q_hbm.shape[0], q_ref, 0),
        (kc_hbm, 0, cached, k_ref, 0),
        (near_hbm, 0, half, k_ref, cached),
        (far_hbm, 0, half, k_ref, cached + half),
        (vc_hbm, 0, cached, v_ref, 0),
        (near_hbm, half, half, v_ref, cached),
        (far_hbm, half, half, v_ref, cached + half),
    ]
    groups = [(0, 1), (1, heads)] if heads > 1 else [(0, 1)]
    copies = []
    for g, (low, high) in enumerate(groups):
        here = slice(low * HD, high * HD)
        there = slice((start + low) * HD, (start + high) * HD)
        copies.append(
            [
                pltpu.make_async_copy(
                    src.at[at : at + size, there], dst.at[to : to + size, here], sems.at[g, n]
                )
                for n, (src, at, size, dst, to) in enumerate(moves)
            ]
        )
        for copy in copies[g]:
            copy.start()
    total = own_sq[0:1, :] + far_sq[0:1, :]
    inverse = lax.rsqrt(total / width + EPSILON)
    inverse = jnp.broadcast_to(inverse, (HD, inverse.shape[1])).T
    penalty = jnp.where(owner_ref[0] == 1, F32(OUT), F32(0.0))
    s_refs, p_refs = (s_a, s_b), (p_a, p_b)
    tiles = tiles_of(keys, cached)
    bases, masses = {}, {}
    for t in range(heads + 2):
        to_score, to_soften, to_gather = t, t - 1, t - 2
        scoring, softening, gathering = t < heads, 0 <= t - 1 < heads, t - 2 >= 0
        if t < len(groups):
            for copy in copies[t]:
                copy.wait()
        if scoring:
            cols = slice(to_score * HD, (to_score + 1) * HD)
            normed = (q_ref[:, cols].astype(F32) * inverse * gain_ref[:, cols]).astype(BF16)
            top = None
        value, mass = None, None
        for at, size, masked in tiles:
            span = slice(at, at + size)
            if gathering:
                part = lax.dot_general(
                    v_ref[span, to_gather * HD : (to_gather + 1) * HD],
                    p_refs[to_gather % 2][span, :],
                    TN,
                    preferred_element_type=F32,
                )
                value = part if value is None else value + part
            if scoring:
                scores = lax.dot_general(k_ref[span, cols], normed, NT, preferred_element_type=F32)
                s_refs[to_score % 2][span, :] = scores
                most = by_eight(jnp.max, scores)
                if masked:
                    most = most + penalty
                top = most if top is None else jnp.maximum(top, most)
            if softening:
                base = bases[to_soften]
                shift = base - penalty if masked else base
                raw = jnp.exp2(s_refs[to_soften % 2][span, :] * scale - shift)
                p_refs[to_soften % 2][span, :] = raw.astype(BF16)
                sums = by_eight(jnp.sum, raw)
                mass = sums if mass is None else mass + sums
        if gathering:
            at = slice(to_gather * HD, (to_gather + 1) * HD)
            out_ref[at, :] = (value * (1.0 / masses[to_gather])).astype(BF16)
        if softening:
            mass = jnp.sum(mass, axis=0, keepdims=True)
            masses[to_soften] = mass
            lse_s[to_soften : to_soften + 1, :] = bases[to_soften] + jnp.log2(mass)
        if scoring:
            bases[to_score] = jnp.max(top, axis=0, keepdims=True) * scale
    out_ref[heads * HD :, :] = split(lse_s[0:heads, :])


def split(lse):
    high = lse.astype(BF16).astype(F32)
    rest = lse - high
    mid = rest.astype(BF16).astype(F32)
    low = rest - mid
    pad = jnp.zeros((STATS - 3 * lse.shape[0], lse.shape[1]), F32)
    return jnp.concatenate([high, mid, low, pad], axis=0).astype(BF16)


def attend(start, heads, width, is_owner, queries, gain, own_sq, far_sq, kc, vc, near, far):
    rows = queries.shape[0]
    keys = kc.shape[0] + near.shape[0]
    wide = heads * HD
    return pl.pallas_call(
        functools.partial(attend_kernel, start, heads, width),
        out_shape=jax.ShapeDtypeStruct((wide + STATS, rows), BF16),
        in_specs=[pl.BlockSpec(memory_space=pltpu.SMEM)] + [vmem()] * 2 + [hbm()] * 5 + [anywhere()],
        out_specs=vmem(),
        scratch_shapes=[pltpu.VMEM((8, rows), F32)]
        + [pltpu.VMEM((keys, rows), F32)] * 2
        + [pltpu.VMEM((keys, rows), BF16)] * 2
        + [pltpu.VMEM((1, wide), F32), pltpu.VMEM((rows, wide), BF16)]
        + [pltpu.VMEM((keys, wide), BF16)] * 2
        + [pltpu.SemaphoreType.DMA((2, 8))],
        cost_estimate=pl.CostEstimate(
            flops=16 * heads * rows * keys * HD,
            bytes_accessed=4 * heads * keys * HD,
            transcendentals=heads * rows * keys,
        ),
        compiler_params=pltpu.CompilerParams(vmem_limit_bytes=12 << 20),
        name="attend",
    )(is_owner, own_sq, far_sq, gain, queries, kc, vc, near, far)


def stats_of(ref, heads):
    stats = ref[heads * HD :, :].astype(F32)
    return stats[:heads] + stats[heads : 2 * heads] + stats[2 * heads : 3 * heads]


def merge_kernel(heads, guarded, *refs):
    own, got, out_ref = refs[-3:]
    own_lse, got_lse = stats_of(own, heads), stats_of(got, heads)
    if guarded:
        got_lse = jnp.where(refs[0][0] == 1, got_lse, F32(OUT))
    top = jnp.maximum(own_lse, got_lse)
    own_w, got_w = jnp.exp2(own_lse - top), jnp.exp2(got_lse - top)
    mass = own_w + got_w
    share = 1.0 / mass
    own_w, got_w = own_w * share, got_w * share
    for h in range(heads):
        at = slice(h * HD, (h + 1) * HD)
        mixed = own[at, :].astype(F32) * own_w[h : h + 1] + got[at, :].astype(F32) * got_w[h : h + 1]
        out_ref[at, :] = mixed.astype(BF16)
    out_ref[heads * HD :, :] = split(top + jnp.log2(mass))


def merge(heads, take, own, got):
    guard = [] if take is None else [take.astype(jnp.int32)[None]]
    return pl.pallas_call(
        functools.partial(merge_kernel, heads, bool(guard)),
        out_shape=jax.ShapeDtypeStruct(own.shape, BF16),
        in_specs=[pl.BlockSpec(memory_space=pltpu.SMEM)] * len(guard) + [vmem()] * 2,
        out_specs=vmem(),
        cost_estimate=pl.CostEstimate(
            flops=4 * own.size, bytes_accessed=6 * own.size, transcendentals=0
        ),
        compiler_params=pltpu.CompilerParams(vmem_limit_bytes=4 << 20),
        name="merge",
    )(*guard, own, got)


def project_kernel(bounds, before, more, *refs):
    attended_ref, weight_hbm = refs[:2]
    sum_ref, turned, weight, sems = refs[2 + before], *refs[-3:]
    first, cols = bounds[0], sum_ref.shape[1]
    spans = [slice(low, high) for low, high in zip(bounds[:-1], bounds[1:])]
    places = [slice(span.start - first, span.stop - first) for span in spans]
    copies = [
        pltpu.make_async_copy(weight_hbm.at[span, :], weight.at[place, :], sems.at[n])
        for n, (span, place) in enumerate(zip(spans, places))
    ]
    if more:
        later_ref = refs[3 + before]
        copies.append(
            pltpu.make_async_copy(
                weight_hbm.at[bounds[-1] : bounds[-1] + more, :], later_ref, sems.at[len(spans)]
            )
        )
    for copy in copies:
        copy.start()
    turned[...] = attended_ref[...].T
    for n, place in enumerate(places):
        copies[n].wait()
        for low in range(0, cols, 256):
            tile = slice(low, min(low + 256, cols))
            term = jnp.dot(turned[:, place], weight[place, tile], preferred_element_type=F32)
            if n or before:
                term = term + (sum_ref if n else refs[2])[:, tile]
            sum_ref[:, tile] = term
    if more:
        copies[-1].wait()


def project(bounds, more, attended, weight, before):
    depth, rows = attended.shape
    cols = weight.shape[1]
    before = [] if before is None else [before]
    shapes = [jax.ShapeDtypeStruct((rows, cols), F32)]
    if more:
        shapes.append(jax.ShapeDtypeStruct((more, cols), BF16))
    return pl.pallas_call(
        functools.partial(project_kernel, bounds, len(before), more),
        out_shape=shapes,
        in_specs=[vmem(), hbm()] + [vmem()] * len(before),
        out_specs=[vmem()] * len(shapes),
        scratch_shapes=[
            pltpu.VMEM((rows, depth), BF16),
            pltpu.VMEM((depth, cols), BF16),
            pltpu.SemaphoreType.DMA((len(bounds),)),
        ],
        cost_estimate=pl.CostEstimate(
            flops=2 * depth * rows * cols, bytes_accessed=2 * depth * cols, transcendentals=0
        ),
        compiler_params=pltpu.CompilerParams(vmem_limit_bytes=16 << 20),
        name="project",
    )(attended, weight, *before)


def finish_kernel(at_ref, attended_ref, weight_ref, sum_ref, out_ref):
    turned = attended_ref[...].T
    cols = out_ref.shape[1]
    for low in range(0, cols, 256):
        wide = min(256, cols - low)
        tile = pl.ds(pl.multiple_of(at_ref[0] * HD + low, HD), wide)
        term = jnp.dot(turned, weight_ref[:, tile], preferred_element_type=F32)
        out_ref[:, low : low + wide] = (sum_ref[:, tile] + term).astype(out_ref.dtype)


def finish(at, cols, dtype, attended, weight, summed):
    return pl.pallas_call(
        finish_kernel,
        out_shape=jax.ShapeDtypeStruct((summed.shape[0], cols), dtype),
        in_specs=[pl.BlockSpec(memory_space=pltpu.SMEM)] + [vmem()] * 3,
        out_specs=vmem(),
        cost_estimate=pl.CostEstimate(
            flops=2 * attended.size * cols, bytes_accessed=2 * weight.size, transcendentals=0
        ),
        compiler_params=pltpu.CompilerParams(vmem_limit_bytes=12 << 20),
        name="finish",
    )(at, attended, weight, summed)


def local(
    n_slab, n_head, n_seq,
    queries, query_gain, cache_keys, cache_values, finished_keys, finished_values,
    new_keys, new_values, out_weight, time_weight, owner, step,
):
    queries, cache_keys, cache_values, finished_keys, finished_values, new_keys, new_values = in_hbm(
        queries, cache_keys, cache_values, finished_keys, finished_values, new_keys, new_values
    )
    (out_weight,) = in_hbm(out_weight)
    heads = queries.shape[1] // HD
    width = queries.shape[1] * n_head
    slab = lax.axis_index("slab")

    own_sq, near = prepare(queries, finished_keys, new_keys, finished_values, new_values)
    if n_head == 2:
        far_sq = lax.ppermute(own_sq, "head", [(0, 1), (1, 0)])
    else:
        far_sq = lax.psum(own_sq, "head")
        own_sq = jnp.zeros_like(own_sq)
    far = lax.ppermute(near, "seq", [(0, 1), (1, 0)])
    is_owner = (slab == owner).astype(jnp.int32)
    gain = query_gain[None, :]
    first_far = far
    gain, near, far = in_hbm(gain, near, far)

    sizes = chunk_sizes(heads)
    starts = [sum(sizes[:c]) for c in range(len(sizes))]
    count = len(sizes)
    side = n_slab // 2
    outer = functools.reduce(jnp.logical_or, [(slab < side - 1), (slab > side)])
    inward = [[(j, j + 1), (n_slab - 1 - j, n_slab - 2 - j)] for j in range(side - 1)]
    outward = [[(b, a) for a, b in pairs] for pairs in inward]
    own, got_in, folded, crossed, total, final = {}, {}, {}, {}, {}, {}
    last, early_sum, arrived = [], [], []

    def run(value):
        last[:] = [value]
        return value

    def attention(c):
        flag = in_order(is_owner, *last)
        own[c] = run(
            attend(
                starts[c], sizes[c], width, flag, queries, gain, own_sq,
                far_sq, cache_keys, cache_values, near, far if c else first_far,
            )
        )

    def send_in(c):
        sent = own[c]
        for j in range(side - 2):
            got = lax.ppermute(sent, "slab", inward[j])
            take = (slab == j + 1) | (slab == n_slab - 2 - j)
            sent = merge(sizes[c], take, sent, got)
        own[c] = sent
        got_in[c] = lax.ppermute(sent, "slab", inward[side - 2]) if side > 1 else sent

    def fold(c):
        take = ((slab == side - 1) | (slab == side)) if side != 2 else None
        got = in_order(got_in[c], *last)
        folded[c] = run(merge(sizes[c], take, own[c], got))
        crossed[c] = lax.ppermute(folded[c], "slab", [(side - 1, side), (side, side - 1)])

    def cross(c):
        got = in_order(crossed[c], *last)
        total[c] = run(merge(sizes[c], None, folded[c], got))

    def send_out(c):
        attended = total[c][: sizes[c] * HD]
        for j in range(side - 2, -1, -1):
            got = lax.ppermute(attended, "slab", outward[j])
            if c == count - 1 and j == 0:
                arrived.append(got)
            else:
                attended = jnp.where((slab == j) | (slab == n_slab - 1 - j), got, attended)
        final[c] = attended

    def project_early(c):
        parts = range(c + 1)
        bounds = tuple(start * HD for start in starts[: c + 2])
        early = jnp.concatenate([final[p] for p in parts], axis=0)
        (summed,) = project(bounds, 0, in_order(early, *last), out_weight, None)
        early_sum.append(run(summed))

    def send_both(c):
        if side != 2:
            send_in(c)
            send_out(c - 3)
            return
        rows = max(own[c].shape[0], total[c - 3].shape[0])
        going, coming = (
            jnp.pad(m, ((0, rows - m.shape[0]), (0, 0))) for m in (own[c], total[c - 3])
        )
        sent = run(jnp.where(outer, going, coming))
        got = lax.ppermute(sent, "slab", inward[0] + outward[0])
        got_in[c] = got[: own[c].shape[0]]
        final[c - 3] = jnp.where(outer, got, sent)[: sizes[c - 3] * HD]

    steps = {"A": attention, "I": send_in, "F": fold, "C": cross, "O": send_out, "X": send_both}
    steps["P"] = project_early
    for kind, c in order_of(sizes):
        steps[kind](c)
    bounds = tuple(start * HD for start in starts[count - 2 :])
    projected, later = project(
        bounds, sizes[-1] * HD, in_order(final[count - 2], *last), out_weight,
        early_sum[0] if early_sum else None,
    )
    attended = final[count - 1]
    if arrived:
        got = in_order(arrived[0], projected)
        attended = jnp.where((slab == 0) | (slab == n_slab - 1), got, attended)

    half = time_weight.shape[0] // 2
    frequency = jnp.exp(-jnp.log(10000.0) * jnp.arange(half, dtype=F32) / half)
    phases = step[0].astype(F32) * frequency
    embedding = jnp.concatenate([jnp.cos(phases), jnp.sin(phases)])
    time_gate = 1.0 + jnp.dot(embedding, time_weight, precision=lax.Precision.HIGHEST)

    cols = time_weight.shape[1]
    if n_head == 2 and cols % HD == 0:
        mine = lax.axis_index("head") * (cols // HD)
        other = (cols // HD) - mine
        sent = finish(other[None], cols, BF16, attended, later, projected)
        got = lax.ppermute(sent, "head", [(0, 1), (1, 0)])
        kept = finish(mine[None], cols, F32, in_order(attended, sent), later, projected)
        summed = kept + got.astype(F32)
    else:
        zero = jnp.zeros((1,), jnp.int32)
        ready = finish(zero, projected.shape[1], F32, attended, later, projected)
        summed = lax.psum_scatter(ready, "head", scatter_dimension=1, tiled=True)
    return (time_gate * summed).astype(BF16)


def solution(mesh):
    in_specs = (
        P(("grp", "seq"), "head"),
        P("head"),
        P(("grp", "slab"), "head"),
        P(("grp", "slab"), "head"),
        P(("grp", "slab", "seq"), "head"),
        P(("grp", "slab", "seq"), "head"),
        P(("grp", "slab", "seq"), "head"),
        P(("grp", "slab", "seq"), "head"),
        P("head", "slab"),
        P(None, ("slab", "head")),
        P("grp"),
        P("grp"),
    )
    out_specs = P(("grp", "seq"), ("slab", "head"))

    def body(*arrays):
        return local(*sizes, *arrays)

    sizes = mesh.shape["slab"], mesh.shape["head"], mesh.shape["seq"]
    return jax.shard_map(body, mesh=mesh, in_specs=in_specs, out_specs=out_specs, check_vma=False)
```

```python
import functools

import jax
import jax.numpy as jnp
from jax import lax
from jax.experimental import pallas as pl
from jax.experimental.pallas import tpu as pltpu
from jax.sharding import PartitionSpec as P


HD = 128
EPSILON = 1e-06
LOG2E = 1.4426950408889634
OUT = -1e30
F32 = jnp.float32
BF16 = jnp.bfloat16
STATS = 16


def chunk_sizes(heads):
    count = -(-heads // 4) if heads > 4 else 2
    sizes = [heads // count + (c < heads % count) for c in range(count)]
    if count > 3:
        sizes[0], sizes[1] = sizes[0] - 1, sizes[1] + 1
    return sizes


def order_of(sizes):
    count = len(sizes)
    if count < 3:
        steps = [(kind, c) for c in range(count) for kind in "AI"]
        steps += [("F", c) for c in range(count)]
        return steps + [(kind, c) for c in range(count) for kind in "CO"]
    steps = [(kind, c) for c in range(3) for kind in "AI"] + [("F", 0)]
    for c in range(3, count):
        steps += [("A", c), ("F", c - 2), ("C", c - 3)]
        steps += [("X", c)]
    for c in range(max(count - 3, 0), count):
        if c + 1 < count:
            steps += [("F", c + 1)]
        steps += [("C", c), ("O", c)]
    return steps


def in_order(value, *earlier):
    return lax.optimization_barrier((value, *earlier))[0]


def vmem():
    return pl.BlockSpec(memory_space=pltpu.VMEM)


def hbm():
    return pl.BlockSpec(memory_space=pltpu.HBM)


def anywhere():
    return pl.BlockSpec(memory_space=pl.ANY)


def in_hbm(*arrays):
    return [pltpu.with_memory_space_constraint(array, pltpu.HBM) for array in arrays]


def prepare_kernel(q_hbm, fk, nk, fv, nv, squares_ref, near_ref, q_ref, sems):
    rows = fk.shape[0]
    heads = q_ref.shape[1] // HD
    pieces = [slice(c * 5 * HD, min((c + 1) * 5, heads) * HD) for c in range(-(-heads // 5))]
    loads = [
        pltpu.make_async_copy(q_hbm.at[:, piece], q_ref.at[:, piece], sems.at[n + 4])
        for n, piece in enumerate(pieces)
    ]
    copies = [
        pltpu.make_async_copy(src, near_ref.at[pl.ds(n * rows, rows), :], sems.at[n])
        for n, src in enumerate((fk, nk, fv, nv))
    ]
    for copy in loads + copies:
        copy.start()
    total = None
    for h in range(heads):
        if h % 5 == 0:
            loads[h // 5].wait()
        block = q_ref[:, h * HD : (h + 1) * HD].astype(F32)
        term = block * block
        total = term if total is None else total + term
    row = jnp.sum(total.T, axis=0, keepdims=True)
    squares_ref[...] = jnp.broadcast_to(row, squares_ref.shape)
    for copy in copies:
        copy.wait()


def prepare(queries, fk, nk, fv, nv):
    rows = queries.shape[0]
    return pl.pallas_call(
        prepare_kernel,
        out_shape=(
            jax.ShapeDtypeStruct((8, rows), F32),
            jax.ShapeDtypeStruct((4 * fk.shape[0], fk.shape[1]), BF16),
        ),
        in_specs=[hbm()] * 5,
        out_specs=(vmem(), vmem()),
        scratch_shapes=[pltpu.VMEM(queries.shape, BF16), pltpu.SemaphoreType.DMA((4 + -(-queries.shape[1] // (5 * HD)),))],
        cost_estimate=pl.CostEstimate(
            flops=2 * queries.size, bytes_accessed=8 * queries.size, transcendentals=0
        ),
        compiler_params=pltpu.CompilerParams(vmem_limit_bytes=8 << 20),
        name="prepare",
    )(queries, fk, nk, fv, nv)


NT = (((1,), (1,)), ((), ()))
TN = (((0,), (0,)), ((), ()))


def tiles_of(keys, cached, size=256):
    tiles, at = [], 0
    for end in (cached, keys):
        while at < end:
            step = min(size, end - at)
            tiles.append((at, step, end == cached))
            at += step
    return tiles


def by_eight(op, array):
    return op(array.reshape(array.shape[0] // 8, 8, array.shape[1]), axis=0)


def attend_kernel(
    start, heads, width, owner_ref, own_sq, far_sq, gain_hbm, q_hbm, kc_hbm, vc_hbm, near_hbm,
    far_hbm, out_ref, lse_s, s_a, s_b, p_a, p_b, gain_ref, q_ref, k_ref, v_ref, sems,
):
    half = near_hbm.shape[0] // 2
    cached, keys = kc_hbm.shape[0], k_ref.shape[0]
    scale = LOG2E / HD**0.5
    moves = [
        (gain_hbm, 0, gain_hbm.shape[0], gain_ref, 0),
        (q_hbm, 0, q_hbm.shape[0], q_ref, 0),
        (kc_hbm, 0, cached, k_ref, 0),
        (near_hbm, 0, half, k_ref, cached),
        (far_hbm, 0, half, k_ref, cached + half),
        (vc_hbm, 0, cached, v_ref, 0),
        (near_hbm, half, half, v_ref, cached),
        (far_hbm, half, half, v_ref, cached + half),
    ]
    groups = [(0, 1), (1, heads)] if heads > 1 else [(0, 1)]
    copies = []
    for g, (low, high) in enumerate(groups):
        here = slice(low * HD, high * HD)
        there = slice((start + low) * HD, (start + high) * HD)
        copies.append(
            [
                pltpu.make_async_copy(
                    src.at[at : at + size, there], dst.at[to : to + size, here], sems.at[g, n]
                )
                for n, (src, at, size, dst, to) in enumerate(moves)
            ]
        )
        for copy in copies[g]:
            copy.start()
    total = own_sq[0:1, :] + far_sq[0:1, :]
    inverse = lax.rsqrt(total / width + EPSILON)
    inverse = jnp.broadcast_to(inverse, (HD, inverse.shape[1])).T
    penalty = jnp.where(owner_ref[0] == 1, F32(OUT), F32(0.0))
    s_refs, p_refs = (s_a, s_b), (p_a, p_b)
    tiles = tiles_of(keys, cached)
    bases, masses = {}, {}
    for t in range(heads + 2):
        to_score, to_soften, to_gather = t, t - 1, t - 2
        scoring, softening, gathering = t < heads, 0 <= t - 1 < heads, t - 2 >= 0
        if t < len(groups):
            for copy in copies[t]:
                copy.wait()
        if scoring:
            cols = slice(to_score * HD, (to_score + 1) * HD)
            normed = (q_ref[:, cols].astype(F32) * inverse * gain_ref[:, cols]).astype(BF16)
            top = None
        value, mass = None, None
        for at, size, masked in tiles:
            span = slice(at, at + size)
            if gathering:
                part = lax.dot_general(
                    v_ref[span, to_gather * HD : (to_gather + 1) * HD],
                    p_refs[to_gather % 2][span, :],
                    TN,
                    preferred_element_type=F32,
                )
                value = part if value is None else value + part
            if scoring:
                scores = lax.dot_general(k_ref[span, cols], normed, NT, preferred_element_type=F32)
                s_refs[to_score % 2][span, :] = scores
                most = by_eight(jnp.max, scores)
                if masked:
                    most = most + penalty
                top = most if top is None else jnp.maximum(top, most)
            if softening:
                base = bases[to_soften]
                shift = base - penalty if masked else base
                raw = jnp.exp2(s_refs[to_soften % 2][span, :] * scale - shift)
                p_refs[to_soften % 2][span, :] = raw.astype(BF16)
                sums = by_eight(jnp.sum, raw)
                mass = sums if mass is None else mass + sums
        if gathering:
            at = slice(to_gather * HD, (to_gather + 1) * HD)
            out_ref[at, :] = (value * (1.0 / masses[to_gather])).astype(BF16)
        if softening:
            mass = jnp.sum(mass, axis=0, keepdims=True)
            masses[to_soften] = mass
            lse_s[to_soften : to_soften + 1, :] = bases[to_soften] + jnp.log2(mass)
        if scoring:
            bases[to_score] = jnp.max(top, axis=0, keepdims=True) * scale
    out_ref[heads * HD :, :] = split(lse_s[0:heads, :])


def split(lse):
    high = lse.astype(BF16).astype(F32)
    rest = lse - high
    mid = rest.astype(BF16).astype(F32)
    low = rest - mid
    pad = jnp.zeros((STATS - 3 * lse.shape[0], lse.shape[1]), F32)
    return jnp.concatenate([high, mid, low, pad], axis=0).astype(BF16)


def attend(start, heads, width, is_owner, queries, gain, own_sq, far_sq, kc, vc, near, far):
    rows = queries.shape[0]
    keys = kc.shape[0] + near.shape[0]
    wide = heads * HD
    return pl.pallas_call(
        functools.partial(attend_kernel, start, heads, width),
        out_shape=jax.ShapeDtypeStruct((wide + STATS, rows), BF16),
        in_specs=[pl.BlockSpec(memory_space=pltpu.SMEM)] + [vmem()] * 2 + [hbm()] * 5 + [anywhere()],
        out_specs=vmem(),
        scratch_shapes=[pltpu.VMEM((8, rows), F32)]
        + [pltpu.VMEM((keys, rows), F32)] * 2
        + [pltpu.VMEM((keys, rows), BF16)] * 2
        + [pltpu.VMEM((1, wide), F32), pltpu.VMEM((rows, wide), BF16)]
        + [pltpu.VMEM((keys, wide), BF16)] * 2
        + [pltpu.SemaphoreType.DMA((2, 8))],
        cost_estimate=pl.CostEstimate(
            flops=16 * heads * rows * keys * HD,
            bytes_accessed=4 * heads * keys * HD,
            transcendentals=heads * rows * keys,
        ),
        compiler_params=pltpu.CompilerParams(vmem_limit_bytes=12 << 20),
        name="attend",
    )(is_owner, own_sq, far_sq, gain, queries, kc, vc, near, far)


def stats_of(ref, heads):
    stats = ref[heads * HD :, :].astype(F32)
    return stats[:heads] + stats[heads : 2 * heads] + stats[2 * heads : 3 * heads]


def merge_kernel(heads, guarded, *refs):
    own, got, out_ref = refs[-3:]
    own_lse, got_lse = stats_of(own, heads), stats_of(got, heads)
    if guarded:
        got_lse = jnp.where(refs[0][0] == 1, got_lse, F32(OUT))
    top = jnp.maximum(own_lse, got_lse)
    own_w, got_w = jnp.exp2(own_lse - top), jnp.exp2(got_lse - top)
    mass = own_w + got_w
    share = 1.0 / mass
    own_w, got_w = own_w * share, got_w * share
    for h in range(heads):
        at = slice(h * HD, (h + 1) * HD)
        mixed = own[at, :].astype(F32) * own_w[h : h + 1] + got[at, :].astype(F32) * got_w[h : h + 1]
        out_ref[at, :] = mixed.astype(BF16)
    out_ref[heads * HD :, :] = split(top + jnp.log2(mass))


def merge(heads, take, own, got):
    guard = [] if take is None else [take.astype(jnp.int32)[None]]
    return pl.pallas_call(
        functools.partial(merge_kernel, heads, bool(guard)),
        out_shape=jax.ShapeDtypeStruct(own.shape, BF16),
        in_specs=[pl.BlockSpec(memory_space=pltpu.SMEM)] * len(guard) + [vmem()] * 2,
        out_specs=vmem(),
        cost_estimate=pl.CostEstimate(
            flops=4 * own.size, bytes_accessed=6 * own.size, transcendentals=0
        ),
        compiler_params=pltpu.CompilerParams(vmem_limit_bytes=4 << 20),
        name="merge",
    )(*guard, own, got)


def project_kernel(bounds, attended_ref, weight_hbm, sum_ref, later_ref, turned, weight, sems):
    depth, cols = attended_ref.shape[0], sum_ref.shape[1]
    parts = len(bounds) - 1
    spans = [slice(low, high) for low, high in zip(bounds[:-1], bounds[1:])]
    copies = [
        pltpu.make_async_copy(weight_hbm.at[span, :], weight.at[span, :], sems.at[n])
        for n, span in enumerate(spans)
    ]
    copies.append(
        pltpu.make_async_copy(
            weight_hbm.at[pl.ds(depth, later_ref.shape[0]), :], later_ref, sems.at[parts]
        )
    )
    for copy in copies:
        copy.start()
    turned[...] = attended_ref[...].T
    for n in range(parts):
        copies[n].wait()
        span = spans[n]
        for low in range(0, cols, 256):
            tile = slice(low, min(low + 256, cols))
            term = jnp.dot(turned[:, span], weight[span, tile], preferred_element_type=F32)
            sum_ref[:, tile] = term if n == 0 else sum_ref[:, tile] + term
    copies[parts].wait()


def project(bounds, attended, weight):
    depth, rows = attended.shape
    cols = weight.shape[1]
    return pl.pallas_call(
        functools.partial(project_kernel, bounds),
        out_shape=(
            jax.ShapeDtypeStruct((rows, cols), F32),
            jax.ShapeDtypeStruct((weight.shape[0] - depth, cols), BF16),
        ),
        in_specs=[vmem(), hbm()],
        out_specs=(vmem(), vmem()),
        scratch_shapes=[
            pltpu.VMEM((rows, depth), BF16),
            pltpu.VMEM((depth, cols), BF16),
            pltpu.SemaphoreType.DMA((len(bounds),)),
        ],
        cost_estimate=pl.CostEstimate(
            flops=2 * depth * rows * cols, bytes_accessed=2 * weight.size, transcendentals=0
        ),
        compiler_params=pltpu.CompilerParams(vmem_limit_bytes=16 << 20),
        name="project",
    )(attended, weight)


def finish_kernel(at_ref, attended_ref, weight_ref, sum_ref, out_ref):
    turned = attended_ref[...].T
    cols = out_ref.shape[1]
    for low in range(0, cols, 256):
        wide = min(256, cols - low)
        tile = pl.ds(pl.multiple_of(at_ref[0] * HD + low, HD), wide)
        term = jnp.dot(turned, weight_ref[:, tile], preferred_element_type=F32)
        out_ref[:, low : low + wide] = (sum_ref[:, tile] + term).astype(out_ref.dtype)


def finish(at, cols, dtype, attended, weight, summed):
    return pl.pallas_call(
        finish_kernel,
        out_shape=jax.ShapeDtypeStruct((summed.shape[0], cols), dtype),
        in_specs=[pl.BlockSpec(memory_space=pltpu.SMEM)] + [vmem()] * 3,
        out_specs=vmem(),
        cost_estimate=pl.CostEstimate(
            flops=2 * attended.size * cols, bytes_accessed=2 * weight.size, transcendentals=0
        ),
        compiler_params=pltpu.CompilerParams(vmem_limit_bytes=12 << 20),
        name="finish",
    )(at, attended, weight, summed)


def local(
    n_slab, n_head, n_seq,
    queries, query_gain, cache_keys, cache_values, finished_keys, finished_values,
    new_keys, new_values, out_weight, time_weight, owner, step,
):
    queries, cache_keys, cache_values, finished_keys, finished_values, new_keys, new_values = in_hbm(
        queries, cache_keys, cache_values, finished_keys, finished_values, new_keys, new_values
    )
    (out_weight,) = in_hbm(out_weight)
    heads = queries.shape[1] // HD
    width = queries.shape[1] * n_head
    slab = lax.axis_index("slab")

    own_sq, near = prepare(queries, finished_keys, new_keys, finished_values, new_values)
    if n_head == 2:
        far_sq = lax.ppermute(own_sq, "head", [(0, 1), (1, 0)])
    else:
        far_sq = lax.psum(own_sq, "head")
        own_sq = jnp.zeros_like(own_sq)
    far = lax.ppermute(near, "seq", [(0, 1), (1, 0)])
    is_owner = (slab == owner).astype(jnp.int32)
    gain = query_gain[None, :]
    first_far = far
    gain, near, far = in_hbm(gain, near, far)

    sizes = chunk_sizes(heads)
    starts = [sum(sizes[:c]) for c in range(len(sizes))]
    count = len(sizes)
    side = n_slab // 2
    outer = functools.reduce(jnp.logical_or, [(slab < side - 1), (slab > side)])
    inward = [[(j, j + 1), (n_slab - 1 - j, n_slab - 2 - j)] for j in range(side - 1)]
    outward = [[(b, a) for a, b in pairs] for pairs in inward]
    own, got_in, folded, crossed, total, final = {}, {}, {}, {}, {}, {}
    last = []

    def run(value):
        last[:] = [value]
        return value

    def attention(c):
        flag = in_order(is_owner, *last)
        own[c] = run(
            attend(
                starts[c], sizes[c], width, flag, queries, gain, own_sq,
                far_sq, cache_keys, cache_values, near, far if c else first_far,
            )
        )

    def send_in(c):
        sent = own[c]
        for j in range(side - 2):
            got = lax.ppermute(sent, "slab", inward[j])
            take = (slab == j + 1) | (slab == n_slab - 2 - j)
            sent = merge(sizes[c], take, sent, got)
        own[c] = sent
        got_in[c] = lax.ppermute(sent, "slab", inward[side - 2]) if side > 1 else sent

    def fold(c):
        take = ((slab == side - 1) | (slab == side)) if side != 2 else None
        got = in_order(got_in[c], *last)
        folded[c] = run(merge(sizes[c], take, own[c], got))
        crossed[c] = lax.ppermute(folded[c], "slab", [(side - 1, side), (side, side - 1)])

    def cross(c):
        got = in_order(crossed[c], *last)
        total[c] = run(merge(sizes[c], None, folded[c], got))

    def send_out(c):
        attended = total[c][: sizes[c] * HD]
        for j in range(side - 2, -1, -1):
            got = lax.ppermute(attended, "slab", outward[j])
            attended = jnp.where((slab == j) | (slab == n_slab - 1 - j), got, attended)
        final[c] = attended

    def send_both(c):
        if side != 2:
            send_in(c)
            send_out(c - 3)
            return
        rows = max(own[c].shape[0], total[c - 3].shape[0])
        going, coming = (
            jnp.pad(m, ((0, rows - m.shape[0]), (0, 0))) for m in (own[c], total[c - 3])
        )
        sent = run(jnp.where(outer, going, coming))
        got = lax.ppermute(sent, "slab", inward[0] + outward[0])
        got_in[c] = got[: own[c].shape[0]]
        final[c - 3] = jnp.where(outer, got, sent)[: sizes[c - 3] * HD]

    steps = {"A": attention, "I": send_in, "F": fold, "C": cross, "O": send_out, "X": send_both}
    for kind, c in order_of(sizes):
        steps[kind](c)
    early = jnp.concatenate([final[c] for c in range(count - 1)], axis=0)
    bounds = tuple(start * HD for start in starts)
    projected, later = project(bounds, in_order(early, *last), out_weight)
    attended = in_order(final[count - 1], projected)

    half = time_weight.shape[0] // 2
    frequency = jnp.exp(-jnp.log(10000.0) * jnp.arange(half, dtype=F32) / half)
    phases = step[0].astype(F32) * frequency
    embedding = jnp.concatenate([jnp.cos(phases), jnp.sin(phases)])
    time_gate = 1.0 + jnp.dot(embedding, time_weight, precision=lax.Precision.HIGHEST)

    cols = time_weight.shape[1]
    if n_head == 2 and cols % HD == 0:
        mine = lax.axis_index("head") * (cols // HD)
        other = (cols // HD) - mine
        sent = finish(other[None], cols, BF16, attended, later, projected)
        got = lax.ppermute(sent, "head", [(0, 1), (1, 0)])
        kept = finish(mine[None], cols, F32, in_order(attended, sent), later, projected)
        summed = kept + got.astype(F32)
    else:
        zero = jnp.zeros((1,), jnp.int32)
        ready = finish(zero, projected.shape[1], F32, attended, later, projected)
        summed = lax.psum_scatter(ready, "head", scatter_dimension=1, tiled=True)
    return (time_gate * summed).astype(BF16)


def solution(mesh):
    in_specs = (
        P(("grp", "seq"), "head"),
        P("head"),
        P(("grp", "slab"), "head"),
        P(("grp", "slab"), "head"),
        P(("grp", "slab", "seq"), "head"),
        P(("grp", "slab", "seq"), "head"),
        P(("grp", "slab", "seq"), "head"),
        P(("grp", "slab", "seq"), "head"),
        P("head", "slab"),
        P(None, ("slab", "head")),
        P("grp"),
        P("grp"),
    )
    out_specs = P(("grp", "seq"), ("slab", "head"))

    def body(*arrays):
        return local(*sizes, *arrays)

    sizes = mesh.shape["slab"], mesh.shape["head"], mesh.shape["seq"]
    return jax.shard_map(body, mesh=mesh, in_specs=in_specs, out_specs=out_specs, check_vma=False)
```
